512 devices in a mesh: ctx: 64 (over z, y_lo, core), head: 4 (over x), dp: 2 (over y_hi).
Axes of the slice: x: 4, y: 4 (y_hi: 2, y_lo: 2; y = y_hi * 2 + y_lo), z: 16, core: 2. Of those that a mesh axis runs over, the one named last changes fastest.
Arguments:
- values: bfloat16 [2, 8192, 4096], P('dp', 'ctx', 'head'), may hold values from -6 to 6
- dt_raw: float32 [2, 8192, 64], P('dp', 'ctx', 'head'), may hold values from -4 to 4
- dt_bias: float32 [64], P('head'), may hold values from -8 to -2
- decay_rate: float32 [64], P('head'), may hold values from 0 to 50, as said below
- features: bfloat16 [2, 8192, 8192], P('dp', 'ctx', 'head'), may hold values from -6 to 6
- bc_weight: bfloat16 [8192, 256], P('head'), may hold values from -0.0625 to 0.0625
- out_grad: bfloat16 [2, 8192, 4096], P('dp', 'ctx', 'head'), may hold values from -6 to 6
Outputs:
- grad_values: bfloat16 [2, 8192, 4096], P('dp', 'ctx', 'head')
- grad_dt: float32 [2, 8192, 64], P('dp', 'ctx', 'head')
- grad_features: bfloat16 [2, 8192, 8192], P('dp', 'ctx', 'head')
- grad_weight: float32 [256, 8192], P(('ctx', 'dp'), 'head')
The draws below stay inside these ranges and needn't reach their ends.
Inputs may be any that keep to these rules, and one draw needn't show every extreme that they name: `decay_rate`: positive.
All inputs are finite; a program needn't handle non-finite values.
Results may differ from the reference program's by a relative error of at most 0.014.
Values may be sent and summed in bfloat16 or wider, within the bound.
A program may use at most 192 MiB of HBM per device.

```python
import math
import jax
import jax.numpy as jnp
from jax import lax

D = 8192
P_SIZE = 64
N = 128
TOK_DEV = 128
HEADS = 64
WIDTH = 4096
SEQLEN = 8192
BATCH = 2


def head_params(key):
    pick_key = jax.random.fold_in(key, 11)
    fast_key = jax.random.fold_in(key, 12)
    slow_key = jax.random.fold_in(key, 13)
    mean_key = jax.random.fold_in(key, 14)
    picks = jax.random.randint(pick_key, (HEADS,), 0, 10)
    slow = picks < 5
    fast_step = jnp.exp(jax.random.uniform(fast_key, (HEADS,), jnp.float32, math.log(1.0 / 50.0), math.log(1.0 / 30.0)))
    slow_step = jnp.exp(jax.random.uniform(slow_key, (HEADS,), jnp.float32, math.log(0.2), math.log(1.5))) / SEQLEN
    per_step = jnp.where(slow, slow_step, fast_step)
    step_mean = jnp.exp(jax.random.uniform(mean_key, (HEADS,), jnp.float32, math.log(0.001), math.log(0.1)))
    decay = per_step / step_mean
    offset = jnp.log(jnp.expm1(step_mean))
    return (decay, offset, slow)


def draw_decay_rate(key, part):
    return head_params(key)[0]


def draw_dt_bias(key, part):
    return head_params(key)[1]


def draw_dt_raw(key, part):
    slow = head_params(key)[2]
    blocks = SEQLEN // TOK_DEV
    period_key = jax.random.fold_in(key, 21)
    phase_key = jax.random.fold_in(key, 22)
    spot_key = jax.random.fold_in(key, 23)
    noise_key = jax.random.fold_in(key, 24)
    period = jax.random.randint(period_key, (BATCH, 1, HEADS), 6, 10)
    phase = jax.random.randint(phase_key, (BATCH, 1, HEADS), 0, 10)
    hot_at = jax.random.randint(spot_key, (BATCH, 1, HEADS), 0, blocks)
    block_ids = jax.lax.broadcasted_iota(jnp.int32, (1, blocks, 1), 1)
    where_in = (block_ids + phase) % period
    level = jnp.where(where_in == 0, 2.0, jnp.where(where_in <= period - 2, -3.6, 0.0)).astype(jnp.float32)
    spread = jnp.where(where_in == period - 1, 0.7, 0.2).astype(jnp.float32)
    hot = (block_ids == hot_at) & slow[None, None, :]
    level = jnp.where(hot, 3.8, level)
    spread = jnp.where(hot, 0.2, spread)
    level = jnp.broadcast_to(level[:, :, None, :], (BATCH, blocks, TOK_DEV, HEADS)).reshape(BATCH, SEQLEN, HEADS)
    spread = jnp.broadcast_to(spread[:, :, None, :], (BATCH, blocks, TOK_DEV, HEADS)).reshape(BATCH, SEQLEN, HEADS)
    noise = jax.random.normal(noise_key, (BATCH, SEQLEN, HEADS), jnp.float32)
    return jnp.clip(level + spread * noise, -4.0, 4.0)


def levels(stream_key, extent, shards, smallest, high):
    gain, own = 1.0, jax.random.fold_in(stream_key, 6)
    for dim, blocks in shards:
        draws = jnp.exp(jax.random.uniform(jax.random.fold_in(own, dim), (blocks,), jnp.float32, smallest / len(shards), high / len(shards)))
        gain = gain * jnp.repeat(draws, extent[dim] // blocks).reshape([-1 if axis == dim else 1 for axis in range(len(extent))])
    return gain


def bell_draw(rng, extent, scale, most, cuts=(), held_as=jnp.bfloat16):
    drawn = jax.random.normal(rng, extent, jnp.float32) * scale
    if len(cuts) > 0:
        drawn = levels(rng, extent, cuts, -0.22, 0.18) * drawn
    return jnp.clip(drawn, min=-most, max=most).astype(held_as)


def setup_inputs(seed: int = 0) -> dict:
    arg_keys = jax.random.split(jax.random.key(seed), 8)
    values = bell_draw(arg_keys[0], (BATCH, SEQLEN, WIDTH), 1.0, 6.0, ((0, 2), (1, 64), (2, 4)))
    dt_raw = draw_dt_raw(jax.random.fold_in(arg_keys[7], 71), 0)
    dt_bias = draw_dt_bias(jax.random.fold_in(arg_keys[7], 71), 0)
    decay_rate = draw_decay_rate(jax.random.fold_in(arg_keys[7], 71), 0)
    features = bell_draw(arg_keys[4], (BATCH, SEQLEN, D), 1.0, 6.0, ((0, 2), (1, 64), (2, 4)))
    bc_weight = bell_draw(arg_keys[5], (D, 2 * N), D ** -0.5, 0.0625, ((0, 4),))
    out_grad = bell_draw(arg_keys[6], (BATCH, SEQLEN, WIDTH), 1.0, 6.0, ((0, 2), (1, 64), (2, 4)))
    return dict(values=values, dt_raw=dt_raw, dt_bias=dt_bias, decay_rate=decay_rate, features=features, bc_weight=bc_weight, out_grad=out_grad)


def block_forward(vals_in, raw_in, dt_bias, decay_rate, b_proj, c_proj, state_in):
    step_size = jax.nn.softplus(raw_in + dt_bias[None, :])
    running = jnp.cumsum(-step_size * decay_rate[None, :], axis=0)
    tok_count = vals_in.shape[0]
    row_ids = lax.broadcasted_iota(jnp.int32, (tok_count, tok_count), 0)
    col_ids = lax.broadcasted_iota(jnp.int32, (tok_count, tok_count), 1)
    causal = col_ids <= row_ids
    gap_sums = running.T[:, :, None] - running.T[:, None, :]
    weights = jnp.exp(jnp.where(causal[None, :, :], gap_sums, -1e+30))
    scores = jnp.dot(c_proj, b_proj.T)
    scaled = vals_in * step_size[:, :, None]
    mixing = weights * scores[None, :, :]
    inner_part = jnp.einsum('hts,shp->thp', mixing, scaled)
    carried = jnp.einsum('tn,hpn->thp', c_proj, state_in) * jnp.exp(running)[:, :, None]
    outputs = inner_part + carried
    tail_decay = jnp.exp(running[-1][None, :] - running)
    local_state = jnp.einsum('thp,tn->hpn', scaled * tail_decay[:, :, None], b_proj)
    total_decay = jnp.exp(running[-1])
    state_out = total_decay[:, None, None] * state_in + local_state
    return (outputs, state_out)

def reference(values, dt_raw, dt_bias, decay_rate, features, bc_weight, out_grad):
    blocks = SEQLEN // TOK_DEV

    def one_sequence(inputs):
        vals_seq, raw_seq, feat_seq, grad_seq = inputs
        projected = jnp.dot(feat_seq, bc_weight, preferred_element_type=jnp.float32)
        proj_wide = lax.optimization_barrier(projected.astype(jnp.bfloat16)).astype(jnp.float32)

        def chain(vals_all, raw_all, proj_all):
            vals_blk = vals_all.reshape(blocks, TOK_DEV, HEADS, P_SIZE)
            raw_blk = raw_all.reshape(blocks, TOK_DEV, HEADS)
            b_blk = proj_all[:, :N].reshape(blocks, TOK_DEV, N)
            c_blk = proj_all[:, N:].reshape(blocks, TOK_DEV, N)

            def advance(state, pieces):
                outputs, new_state = block_forward(pieces[0], pieces[1], dt_bias, decay_rate, pieces[2], pieces[3], state)
                return (new_state, outputs)
            start_state = jnp.zeros((HEADS, P_SIZE, N), jnp.float32)
            _, outs = lax.scan(jax.checkpoint(advance), start_state, (vals_blk, raw_blk, b_blk, c_blk))
            return outs.reshape(SEQLEN, HEADS, P_SIZE)
        vals_wide = vals_seq.astype(jnp.float32).reshape(SEQLEN, HEADS, P_SIZE)
        _, pullback = jax.vjp(chain, vals_wide, raw_seq, proj_wide)
        grads_wide = grad_seq.astype(jnp.float32).reshape(SEQLEN, HEADS, P_SIZE)
        value_grad, step_grad, proj_grad = pullback(grads_wide)
        proj_round = proj_grad.astype(jnp.bfloat16)
        grad_feat = jnp.dot(proj_round, bc_weight.T, preferred_element_type=jnp.float32).astype(jnp.bfloat16)
        weight_term = jnp.dot(proj_round.T, feat_seq, preferred_element_type=jnp.float32)
        return (value_grad.reshape(SEQLEN, WIDTH).astype(jnp.bfloat16), step_grad, grad_feat, weight_term)
    grad_values, grad_dt, grad_features, weight_terms = lax.map(one_sequence, (values, dt_raw, features, out_grad))
    return (grad_values, grad_dt, grad_features, lax.optimization_barrier(jnp.sum(weight_terms, axis=0)))
```

```python
import jax
import jax.numpy as jnp
from jax import lax
from jax.experimental import pallas as pl
from jax.experimental.pallas import tpu as pltpu
from jax.sharding import PartitionSpec as P

F32 = jnp.float32
BF16 = jnp.bfloat16
MESH_ID = pl.DeviceIdType.MESH
VMEM = pl.BlockSpec(memory_space=pltpu.VMEM)


def remote(src, dst, send_sem, recv_sem, where):
    return pltpu.make_async_remote_copy(
        src_ref=src, dst_ref=dst, send_sem=send_sem, recv_sem=recv_sem,
        device_id=where, device_id_type=MESH_ID,
    )


def greet(barrier, where):
    pl.semaphore_signal(barrier, inc=1, device_id=where, device_id_type=MESH_ID)


def far_first(k, nz):
    return nz // 2 + (1 - 2 * (k % 2)) * ((k + 1) // 2)


def head_sum_kernel(part_ref, out_ref, got, send, recv):
    me = lax.axis_index("head")
    nh = lax.axis_size("head")
    barrier = pltpu.get_barrier_semaphore()
    for d in range(1, nh):
        greet(barrier, {"head": (me + d) % nh})
    pl.semaphore_wait(barrier, nh - 1)
    copies = []
    for d in (2, 1, 3):
        copies.append(
            remote(part_ref, got.at[d - 1], send.at[d - 1], recv.at[d - 1], {"head": (me + d) % nh})
        )
        copies[-1].start()
    total = part_ref[...].astype(F32)
    for copy in copies:
        copy.wait_recv()
    for d in range(nh - 1):
        total = total + got[d].astype(F32)
    out_ref[...] = total.astype(BF16)
    for copy in copies:
        copy.wait_send()


def head_sum(part, which):
    nh = lax.axis_size("head")
    return pl.pallas_call(
        head_sum_kernel,
        out_shape=jax.ShapeDtypeStruct(part.shape, BF16),
        in_specs=[VMEM],
        out_specs=VMEM,
        scratch_shapes=[
            pltpu.VMEM((nh - 1,) + part.shape, BF16),
            pltpu.SemaphoreType.DMA((nh - 1,)),
            pltpu.SemaphoreType.DMA((nh - 1,)),
        ],
        compiler_params=pltpu.CompilerParams(collective_id=which, has_side_effects=True),
        name="head_sum",
    )(part)


def scan_kernel(sg, logs, out, r1, r1d, zs, zd, r2, r2d, bk, r4, p5, r5,
                s1, s1d, g1, g1d, s2, s2d, g2, g2d, s4, g4, s5, g5):
    ctx = lax.axis_index("ctx")
    nz = lax.axis_size("ctx") // 4
    z, p = ctx // 4, ctx % 4
    rows = 256 // nz
    barrier = pltpu.get_barrier_semaphore()
    for d in range(1, 4):
        greet(barrier, {"ctx": z * 4 + (p + d) % 4})

    def hello(k, _):
        greet(barrier, {"ctx": ((z + far_first(k, nz)) % nz) * 4 + p})
        return 0

    lax.fori_loop(0, nz - 1, hello, 0)
    pl.semaphore_wait(barrier, 3 + nz - 1)

    def to_plane(d):
        q = (p + d) % 4
        where = {"ctx": z * 4 + q}
        lanes = pl.ds(pl.multiple_of(q * 256, 256), 256)
        return (
            remote(sg.at[:, :, lanes], r1.at[p], s1.at[d - 1], g1.at[p], where),
            remote(logs.at[q], r1d.at[p], s1d.at[d - 1], g1d.at[p], where),
        )

    for d in (2, 3, 1):
        for copy in to_plane(d):
            copy.start()
    r1[p] = sg[:, :, pl.ds(pl.multiple_of(p * 256, 256), 256)]
    r1d[p] = logs[p]
    for d in range(1, 4):
        q = (p + d) % 4
        where = {"ctx": z * 4 + q}
        remote(r1.at[q], r1.at[q], s1.at[0], g1.at[q], where).wait_recv()
        remote(r1d.at[q], r1d.at[q], s1d.at[0], g1d.at[q], where).wait_recv()

    whole = r1d[0] + r1d[1] + r1d[2] + r1d[3]
    zd[0] = whole[:, :128]
    zd[1] = whole[:, 128:]
    for half in range(2):
        lanes = slice(128 * half, 128 * half + 128)
        decay = [jnp.exp(r1d[q][:, lanes]) for q in range(4)]
        fwd = r1[0, 0, :, lanes].astype(F32)
        for q in range(1, 4):
            fwd = fwd * decay[q] + r1[q, 0, :, lanes].astype(F32)
        bwd = r1[3, 1, :, lanes].astype(F32)
        for q in (2, 1, 0):
            bwd = bwd * decay[q] + r1[q, 1, :, lanes].astype(F32)
        for j in range(half, nz, 2):
            at = (j // 2) * rows
            zs[j, 0] = fwd[at:at + rows].astype(BF16)
            zs[j, 1] = bwd[at:at + rows].astype(BF16)

    def to_owner(k, _):
        peer = (z + far_first(k, nz)) % nz
        where = {"ctx": peer * 4 + p}
        remote(zs.at[peer], r2.at[z], s2.at[peer], g2.at[z], where).start()
        remote(zd.at[peer % 2], r2d.at[z], s2d.at[peer], g2d.at[z], where).start()
        return 0

    lax.fori_loop(0, nz - 1, to_owner, 0)
    r2[z] = zs[z]
    r2d[z] = zd[z % 2]

    def from_planes(k, _):
        peer = (z + 1 + k) % nz
        where = {"ctx": peer * 4 + p}
        remote(zs.at[peer], r2.at[peer], s2.at[peer], g2.at[peer], where).wait_recv()
        remote(zd.at[peer % 2], r2d.at[peer], s2d.at[peer], g2d.at[peer], where).wait_recv()
        return 0

    lax.fori_loop(0, nz - 1, from_planes, 0)

    carry = jnp.zeros((rows, 128), F32)
    back = jnp.zeros((rows, 128), F32)
    for k in range(nz):
        bk[k, 0] = carry.astype(BF16)
        carry = carry * jnp.exp(r2d[k]) + r2[k, 0].astype(F32)
        m = nz - 1 - k
        bk[m, 1] = back.astype(BF16)
        back = back * jnp.exp(r2d[m]) + r2[m, 1].astype(F32)

    def to_planes(k, _):
        peer = (z + far_first(k, nz)) % nz
        remote(bk.at[peer], r4.at[z], s4.at[peer], g4.at[z], {"ctx": peer * 4 + p}).start()
        return 0

    lax.fori_loop(0, nz - 1, to_planes, 0)
    r4[z] = bk[z]

    def from_owners(k, _):
        peer = (z + 1 + k) % nz
        remote(bk.at[peer], r4.at[peer], s4.at[peer], g4.at[peer], {"ctx": peer * 4 + p}).wait_recv()
        return 0

    lax.fori_loop(0, nz - 1, from_owners, 0)

    for half in range(2):
        lanes = slice(128 * half, 128 * half + 128)
        decay = [jnp.exp(r1d[q][:, lanes]) for q in range(4)]
        for j in range(half, nz, 2):
            span = slice((j // 2) * rows, (j // 2) * rows + rows)
            state = r4[j, 0].astype(F32)
            for q in range(4):
                p5[q, 0, span, lanes] = state.astype(BF16)
                if q < 3:
                    state = state * decay[q] + r1[q, 0, span, lanes].astype(F32)
            grad = r4[j, 1].astype(F32)
            for q in (3, 2, 1, 0):
                p5[q, 1, span, lanes] = grad.astype(BF16)
                if q > 0:
                    grad = grad * decay[q] + r1[q, 1, span, lanes].astype(F32)

    for d in (2, 3, 1):
        q = (p + d) % 4
        remote(p5.at[q], r5.at[p], s5.at[d - 1], g5.at[p], {"ctx": z * 4 + q}).start()
    r5[p] = p5[p]
    for d in range(1, 4):
        q = (p + d) % 4
        remote(p5.at[q], r5.at[q], s5.at[0], g5.at[q], {"ctx": z * 4 + q}).wait_recv()
    for q in range(4):
        out[:, :, 256 * q:256 * q + 256] = r5[q]

    for d in range(1, 4):
        q = (p + d) % 4
        for copy in to_plane(d):
            copy.wait_send()
        remote(p5.at[q], r5.at[p], s5.at[d - 1], g5.at[p], {"ctx": z * 4 + q}).wait_send()

    def sent(k, _):
        peer = (z + 1 + k) % nz
        where = {"ctx": peer * 4 + p}
        remote(zs.at[peer], r2.at[z], s2.at[peer], g2.at[z], where).wait_send()
        remote(zd.at[peer % 2], r2d.at[z], s2d.at[peer], g2d.at[z], where).wait_send()
        remote(bk.at[peer], r4.at[z], s4.at[peer], g4.at[z], where).wait_send()
        return 0

    lax.fori_loop(0, nz - 1, sent, 0)


def scan_exchange(sg, logs):
    nz = lax.axis_size("ctx") // 4
    rows = 256 // nz
    dma = pltpu.SemaphoreType.DMA
    return pl.pallas_call(
        scan_kernel,
        out_shape=jax.ShapeDtypeStruct(sg.shape, BF16),
        in_specs=[VMEM, VMEM],
        out_specs=VMEM,
        scratch_shapes=[
            pltpu.VMEM((4, 2, 128, 256), BF16),
            pltpu.VMEM((4, 1, 256), F32),
            pltpu.VMEM((nz, 2, rows, 128), BF16),
            pltpu.VMEM((2, 1, 128), F32),
            pltpu.VMEM((nz, 2, rows, 128), BF16),
            pltpu.VMEM((nz, 1, 128), F32),
            pltpu.VMEM((nz, 2, rows, 128), BF16),
            pltpu.VMEM((nz, 2, rows, 128), BF16),
            pltpu.VMEM((4, 2, 128, 256), BF16),
            pltpu.VMEM((4, 2, 128, 256), BF16),
            dma((3,)), dma((3,)), dma((4,)), dma((4,)),
            dma((nz,)), dma((nz,)), dma((nz,)), dma((nz,)),
            dma((nz,)), dma((nz,)), dma((3,)), dma((4,)),
        ],
        compiler_params=pltpu.CompilerParams(collective_id=2, has_side_effects=True),
        name="scan_exchange",
    )(sg, logs)


def weight_kernel(gw, out, e1, hs, e2, zs, e3, s1, g1, s2, g2, s3, g3):
    ctx, dp = lax.axis_index("ctx"), lax.axis_index("dp")
    nz = lax.axis_size("ctx") // 4
    width = gw.shape[1]
    block = gw.shape[0] // 8
    z, low, core = ctx // 4, (ctx // 2) % 2, ctx % 2
    y = dp * 2 + low
    other = {"ctx": ctx + 1 - 2 * core}

    def along_y(d):
        to = (y + d) % 4
        return {"ctx": z * 4 + (to % 2) * 2 + core, "dp": to // 2}

    def along_z(peer):
        return {"ctx": peer * 4 + low * 2 + core}

    barrier = pltpu.get_barrier_semaphore()

    def hello(k, _):
        greet(barrier, along_z((z + far_first(k, nz)) % nz))
        return 0

    lax.fori_loop(0, nz - 1, hello, 0)
    for d in (2, 1, 3):
        greet(barrier, along_y(d))
    greet(barrier, other)
    pl.semaphore_wait(barrier, nz - 1 + 3 + 1)

    first = remote(gw.at[pl.ds(pl.multiple_of((1 - core) * 4 * block, 4 * block), 4 * block)],
                   e1, s1, g1, other)
    first.start()
    first.wait_recv()
    mine = pl.multiple_of(core * 4 * block, 4 * block)

    def pair_sum(b):
        here = gw[pl.ds(pl.multiple_of(mine + b * block, block), block), :].astype(F32)
        there = e1[pl.ds(pl.multiple_of(b * block, block), block), :].astype(F32)
        return here + there

    for d in (2, 1, 3):
        b = (y + d) % 4
        hs[d - 1] = pair_sum(b).astype(BF16)
        remote(hs.at[d - 1], e2.at[d - 1], s2.at[d - 1], g2.at[d - 1], along_y(d)).start()
    total = pair_sum(y)
    for d in (1, 3, 2):
        remote(hs.at[d - 1], e2.at[d - 1], s2.at[d - 1], g2.at[d - 1], along_y(d)).wait_recv()
        total = total + e2[d - 1].astype(F32)
    for k in range(nz):
        zs[k] = total[2 * k:2 * k + 2].astype(BF16)

    def to_rows(k, _):
        peer = (z + far_first(k, nz)) % nz
        remote(zs.at[peer], e3.at[z], s3.at[peer], g3.at[z], along_z(peer)).start()
        return 0

    lax.fori_loop(0, nz - 1, to_rows, 0)
    e3[z] = zs[z]

    def from_all(k, _):
        peer = (z + 1 + k) % nz
        remote(zs.at[peer], e3.at[peer], s3.at[peer], g3.at[peer], along_z(peer)).wait_recv()
        return 0

    lax.fori_loop(0, nz - 1, from_all, 0)
    total = e3[0].astype(F32)
    for k in range(1, nz):
        total = total + e3[k].astype(F32)
    out[...] = total

    first.wait_send()
    for d in range(1, 4):
        remote(hs.at[d - 1], e2.at[d - 1], s2.at[d - 1], g2.at[d - 1], along_y(d)).wait_send()

    def sent(k, _):
        peer = (z + 1 + k) % nz
        remote(zs.at[peer], e3.at[z], s3.at[peer], g3.at[z], along_z(peer)).wait_send()
        return 0

    lax.fori_loop(0, nz - 1, sent, 0)


def weight_sum(gw):
    nz = lax.axis_size("ctx") // 4
    rows, width = gw.shape
    block = rows // 8
    dma = pltpu.SemaphoreType.DMA
    return pl.pallas_call(
        weight_kernel,
        out_shape=jax.ShapeDtypeStruct((2, width), F32),
        in_specs=[VMEM],
        out_specs=VMEM,
        scratch_shapes=[
            pltpu.VMEM((4 * block, width), BF16),
            pltpu.VMEM((3, block, width), BF16),
            pltpu.VMEM((3, block, width), BF16),
            pltpu.VMEM((nz, 2, width), BF16),
            pltpu.VMEM((nz, 2, width), BF16),
            dma, dma, dma((3,)), dma((3,)), dma((nz,)), dma((nz,)),
        ],
        compiler_params=pltpu.CompilerParams(collective_id=3, has_side_effects=True),
        name="weight_sum",
    )(gw)


def block_forward(vals_in, raw_in, dt_bias, decay_rate, b_proj, c_proj, state_in):
    step_size = jax.nn.softplus(raw_in + dt_bias[None, :])
    running = jnp.cumsum(-step_size * decay_rate[None, :], axis=0)
    tok_count = vals_in.shape[0]
    row_ids = lax.broadcasted_iota(jnp.int32, (tok_count, tok_count), 0)
    col_ids = lax.broadcasted_iota(jnp.int32, (tok_count, tok_count), 1)
    causal = col_ids <= row_ids
    gap_sums = running.T[:, :, None] - running.T[:, None, :]
    weights = jnp.exp(jnp.where(causal[None, :, :], gap_sums, -1e30))
    scores = jnp.dot(c_proj, b_proj.T)
    scaled = vals_in * step_size[:, :, None]
    mixing = weights * scores[None, :, :]
    inner_part = jnp.einsum("hts,shp->thp", mixing, scaled)
    carried = jnp.einsum("tn,hpn->thp", c_proj, state_in) * jnp.exp(running)[:, :, None]
    outputs = inner_part + carried
    tail_decay = jnp.exp(running[-1][None, :] - running)
    local_state = jnp.einsum("thp,tn->hpn", scaled * tail_decay[:, :, None], b_proj)
    total_decay = jnp.exp(running[-1])
    state_out = total_decay[:, None, None] * state_in + local_state
    return (outputs, state_out)


def per_device(values, dt_raw, dt_bias, decay_rate, features, bc_weight, out_grad):
    tok_count = values.shape[1]
    head_count = dt_raw.shape[2]
    head_width = values.shape[2] // head_count
    state_size = bc_weight.shape[1] // 2
    nz = lax.axis_size("ctx") // 4
    inputs = features[0]
    part_sums = jnp.dot(inputs, bc_weight, preferred_element_type=F32).astype(BF16)
    proj_bf = head_sum(part_sums, 0)
    proj_wide = proj_bf.astype(F32)
    b_proj = proj_bf[:, :state_size]
    c_proj = proj_bf[:, state_size:]
    vals_wide = values[0].astype(F32).reshape(tok_count, head_count, head_width)
    grads_wide = out_grad[0].astype(F32).reshape(tok_count, head_count, head_width)
    raw_steps = dt_raw[0]
    step_size = jax.nn.softplus(raw_steps + dt_bias[None, :])
    running = jnp.cumsum(-step_size * decay_rate[None, :], axis=0)
    tail_decay = jnp.exp(running[-1][None, :] - running)
    wide = head_count * head_width
    vals_in = (vals_wide * (step_size * tail_decay)[:, :, None]).astype(BF16).reshape(tok_count, wide)
    grads_in = (grads_wide * jnp.exp(running)[:, :, None]).astype(BF16).reshape(tok_count, wide)
    over_tokens = (((0,), (0,)), ((), ()))
    local = jnp.stack([
        lax.dot_general(b_proj, vals_in, over_tokens, preferred_element_type=F32).astype(BF16),
        lax.dot_general(c_proj, grads_in, over_tokens, preferred_element_type=F32).astype(BF16),
    ])
    logs = jnp.repeat(running[-1], head_width).reshape(4, 1, 256)
    carried = scan_exchange(local, logs).astype(F32)
    carried = carried.reshape(2, state_size, head_count, head_width).transpose(0, 2, 3, 1)
    state_in, grad_exit = carried[0], carried[1]

    def local_block(vals_in, raw_in, proj_in):
        return block_forward(
            vals_in, raw_in, dt_bias, decay_rate,
            proj_in[:, :state_size], proj_in[:, state_size:], state_in,
        )

    _, pullback = jax.vjp(local_block, vals_wide, raw_steps, proj_wide)
    value_grad, step_grad, proj_part = pullback((grads_wide, grad_exit))
    proj_round = head_sum(proj_part.astype(BF16), 1)
    grad_features = jnp.dot(proj_round, bc_weight.T, preferred_element_type=F32).astype(BF16)
    ordered = proj_round.reshape(tok_count, nz, 2, 2, 2, 2 * state_size // (8 * nz))
    ordered = ordered.transpose(0, 3, 4, 2, 1, 5).reshape(tok_count, 2 * state_size)
    partial = lax.dot_general(ordered, inputs, over_tokens, preferred_element_type=F32).astype(BF16)
    grad_weight = weight_sum(partial)
    grad_values = value_grad.reshape(tok_count, wide).astype(BF16)
    return (grad_values[None], step_grad[None], grad_features[None], grad_weight)


def solution(mesh):
    return jax.shard_map(
        per_device,
        mesh=mesh,
        in_specs=(
            P("dp", "ctx", "head"),
            P("dp", "ctx", "head"),
            P("head"),
            P("head"),
            P("dp", "ctx", "head"),
            P("head", None),
            P("dp", "ctx", "head"),
        ),
        out_specs=(
            P("dp", "ctx", "head"),
            P("dp", "ctx", "head"),
            P("dp", "ctx", "head"),
            P(("ctx", "dp"), "head"),
        ),
        check_vma=False,
    )
```

```python
import jax
import jax.numpy as jnp
from jax import lax
from jax.experimental import pallas as pl
from jax.experimental.pallas import tpu as pltpu
from jax.sharding import PartitionSpec as P

F32 = jnp.float32
BF16 = jnp.bfloat16
EXACT = lax.Precision.HIGHEST
MESH_ID = pl.DeviceIdType.MESH
VMEM = pl.BlockSpec(memory_space=pltpu.VMEM)
DMA = pltpu.SemaphoreType.DMA


def remote(src, dst, send_sem, recv_sem, where):
    return pltpu.make_async_remote_copy(
        src_ref=src, dst_ref=dst, send_sem=send_sem, recv_sem=recv_sem,
        device_id=where, device_id_type=MESH_ID,
    )


def greet(barrier, where):
    pl.semaphore_signal(barrier, inc=1, device_id=where, device_id_type=MESH_ID)


def far_first(k, nz):
    return nz // 2 + (1 - 2 * (k % 2)) * ((k + 1) // 2)


def dot(a, b, ca, cb, precision=None):
    return lax.dot_general(
        a, b, (((ca,), (cb,)), ((), ())), precision=precision, preferred_element_type=F32
    )


def iota(shape, dim):
    return lax.broadcasted_iota(jnp.int32, shape, dim)


def scratch_plan(nz, tokens, heads, feats, two_n):
    rows = 256 // nz
    half = feats // 2
    block = two_n // 8
    wide = heads * 64
    return dict(
        ha=pltpu.VMEM((tokens, two_n), BF16),
        hb=pltpu.VMEM((tokens, two_n), BF16),
        ga=pltpu.VMEM((3, tokens, two_n), BF16),
        gb=pltpu.VMEM((3, tokens, two_n), BF16),
        ha_s=DMA((3,)), ha_r=DMA((3,)), hb_s=DMA((3,)), hb_r=DMA((3,)),
        lg=pltpu.VMEM((4, 1, 256), F32),
        ld=pltpu.VMEM((4, 1, 256), F32),
        zl=pltpu.VMEM((2, 1, 128), F32),
        zd=pltpu.VMEM((nz, 1, 128), F32),
        lg_s=DMA((3,)), lg_r=DMA((4,)), zl_s=DMA((nz,)), zl_r=DMA((nz,)),
        vin=pltpu.VMEM((tokens, wide), BF16),
        gin=pltpu.VMEM((tokens, wide), BF16),
        sg=pltpu.VMEM((2, 128, wide), BF16),
        r1=pltpu.VMEM((2, 4, 128, 256), BF16),
        zs=pltpu.VMEM((2, nz, rows, 128), BF16),
        r2=pltpu.VMEM((2, nz, rows, 128), BF16),
        bk=pltpu.VMEM((2, nz, rows, 128), BF16),
        r4=pltpu.VMEM((2, nz, rows, 128), BF16),
        p5=pltpu.VMEM((2, 4, 128, 256), BF16),
        r5=pltpu.VMEM((2, 4, 128, 256), BF16),
        s1=DMA((2, 3)), g1=DMA((2, 4)), s2=DMA((2, nz)), g2=DMA((2, nz)),
        s4=DMA((2, nz)), g4=DMA((2, nz)), s5=DMA((2, 3)), g5=DMA((2, 4)),
        dx=pltpu.VMEM((tokens, wide), F32),
        drow=pltpu.VMEM((tokens, tokens), F32),
        pt=pltpu.VMEM((two_n, tokens), BF16),
        w0=pltpu.VMEM((2, two_n // 2, half), BF16),
        w1=pltpu.VMEM((2, two_n // 2, half), F32),
        e1=pltpu.VMEM((2, two_n // 2, half), BF16),
        hs=pltpu.VMEM((2, 3, block, half), BF16),
        e2=pltpu.VMEM((2, 3, block, half), BF16),
        ws=pltpu.VMEM((2, nz, 2, half), BF16),
        e3=pltpu.VMEM((2, nz, 2, half), BF16),
        a1=DMA((2,)), b1=DMA((2,)), a2=DMA((2, 3)), b2=DMA((2, 3)),
        a3=DMA((2, nz)), b3=DMA((2, nz)),
    )


def make_kernel(names):
    def kernel(values, raw, bias, rate, features, weight, out_grad,
               grad_values, grad_dt, grad_features, grad_weight, *scratch):
        s = dict(zip(names, scratch))
        step(values, raw, bias, rate, features, weight, out_grad,
             grad_values, grad_dt, grad_features, grad_weight, **s)
    return kernel


def step(values, raw, bias, rate, features, weight, out_grad,
         grad_values, grad_dt, grad_features, grad_weight, *,
         ha, hb, ga, gb, ha_s, ha_r, hb_s, hb_r,
         lg, ld, zl, zd, lg_s, lg_r, zl_s, zl_r,
         vin, gin, sg, r1, zs, r2, bk, r4, p5, r5, s1, g1, s2, g2, s4, g4, s5, g5,
         dx, drow, pt, w0, w1, e1, hs, e2, ws, e3, a1, b1, a2, b2, a3, b3):
    ctx, head, dp = lax.axis_index("ctx"), lax.axis_index("head"), lax.axis_index("dp")
    nz = zd.shape[0]
    z, p = ctx // 4, ctx % 4
    low, core = (ctx // 2) % 2, ctx % 2
    y = dp * 2 + low
    rows = 256 // nz
    tokens, heads = raw.shape
    pairs = heads // 2
    state = 128
    half = features.shape[1] // 2
    block = weight.shape[1] // 8

    def at_head(d):
        return {"head": (head + d) % 4}

    def in_plane(d):
        return {"ctx": z * 4 + (p + d) % 4}

    def along_z(peer):
        return {"ctx": peer * 4 + p}

    def along_y(d):
        to = (y + d) % 4
        return {"ctx": z * 4 + (to % 2) * 2 + core, "dp": to // 2}

    other = {"ctx": ctx + 1 - 2 * core}

    barrier = pltpu.get_barrier_semaphore()

    def hello(k, _):
        greet(barrier, along_z((z + far_first(k, nz)) % nz))
        return 0

    lax.fori_loop(0, nz - 1, hello, 0)
    for d in (2, 1, 3):
        greet(barrier, along_y(d))
        greet(barrier, at_head(d))
        greet(barrier, in_plane(d))

    ha[...] = dot(features[...], weight[...], 1, 0).astype(BF16)

    pre = raw[...] + bias[...]
    dt = jax.nn.softplus(pre)
    lower = (iota((tokens, tokens), 0) >= iota((tokens, tokens), 1)).astype(F32)
    run = dot(lower, -dt * rate[...], 1, 0, EXACT)
    last = run[tokens - 1:tokens, :]
    into = jnp.exp(run)
    tail = jnp.exp(last - run)
    ends = jnp.exp(last)
    run_t = jnp.concatenate([run, jnp.zeros((tokens, 128 - heads), F32)], axis=1).T
    first_half = iota((tokens, 128), 1) < 64

    def spread(cols, j):
        return jnp.where(first_half, cols[:, 2 * j:2 * j + 1], cols[:, 2 * j + 1:2 * j + 2])

    row_half = iota((1, 128), 1) < 64
    for j in range(pairs):
        lg[j // 2, :, 128 * (j % 2):128 * (j % 2) + 128] = jnp.where(
            row_half, last[:, 2 * j:2 * j + 1], last[:, 2 * j + 1:2 * j + 2]
        )
    dt_tail = dt * tail
    for j in range(pairs):
        lanes = slice(128 * j, 128 * j + 128)
        vin[:, lanes] = (values[:, lanes].astype(F32) * spread(dt_tail, j)).astype(BF16)
        gin[:, lanes] = (out_grad[:, lanes].astype(F32) * spread(into, j)).astype(BF16)

    pl.semaphore_wait(barrier, nz - 1 + 9)

    def head_copy(src, dst, ss, rs, d):
        return remote(src, dst.at[d - 1], ss.at[d - 1], rs.at[d - 1], at_head(d))

    for d in (2, 1, 3):
        head_copy(ha, ga, ha_s, ha_r, d).start()
    for d in (2, 3, 1):
        q = (p + d) % 4
        remote(lg.at[q], ld.at[p], lg_s.at[d - 1], lg_r.at[p], in_plane(d)).start()
    ld[p] = lg[p]
    for d in (1, 2, 3):
        q = (p + d) % 4
        remote(lg.at[q], ld.at[q], lg_s.at[d - 1], lg_r.at[q], in_plane(d)).wait_recv()
    whole = ld[0] + ld[1] + ld[2] + ld[3]
    zl[0] = whole[:, :128]
    zl[1] = whole[:, 128:]

    def send_decay(k, _):
        peer = (z + far_first(k, nz)) % nz
        remote(zl.at[peer % 2], zd.at[z], zl_s.at[peer], zl_r.at[z], along_z(peer)).start()
        return 0

    lax.fori_loop(0, nz - 1, send_decay, 0)
    zd[z] = zl[z % 2]

    total = ha[...].astype(F32)
    for d in (1, 3, 2):
        head_copy(ha, ga, ha_s, ha_r, d).wait_recv()
        total = total + ga[d - 1].astype(F32)
    proj = total.astype(BF16)
    b_proj = proj[:, :state]
    c_proj = proj[:, state:]
    proj_wide = proj.astype(F32)
    b_flip = proj_wide[:, :state].T.astype(BF16)
    c_flip = proj_wide[:, state:].T.astype(BF16)

    def plane_copy(src, dst, ss, rs, w, d):
        q = (p + d) % 4
        lanes = pl.ds(pl.multiple_of(q * 256, 256), 256)
        return remote(src.at[w, :, lanes], dst.at[w, p], ss.at[w, d - 1], rs.at[w, p], in_plane(d))

    for w, flip, fed in ((0, b_flip, vin), (1, c_flip, gin)):
        sg[w] = dot(flip, fed[...], 1, 0).astype(BF16)
        for d in (2, 3, 1):
            plane_copy(sg, r1, s1, g1, w, d).start()
        r1[w, p] = sg[w, :, pl.ds(pl.multiple_of(p * 256, 256), 256)]

    def plane_wait(buf, rs, ss, w):
        for d in (1, 3, 2):
            q = (p + d) % 4
            remote(buf.at[w, q], buf.at[w, q], ss.at[w, d - 1], rs.at[w, q], in_plane(d)).wait_recv()

    decays = [jnp.exp(ld[q]) for q in range(4)]

    def combine(w):
        order = (0, 1, 2, 3) if w == 0 else (3, 2, 1, 0)
        for side in range(2):
            lanes = slice(128 * side, 128 * side + 128)
            acc = r1[w, order[0], :, lanes].astype(F32)
            for n, q in enumerate(order[1:]):
                by = decays[q][:, lanes]
                acc = acc * by + r1[w, q, :, lanes].astype(F32)
            for j in range(side, nz, 2):
                at = (j // 2) * rows
                zs[w, j] = acc[at:at + rows].astype(BF16)

    def z_send(src, dst, ss, rs, w):
        def go(k, _):
            peer = (z + far_first(k, nz)) % nz
            remote(src.at[w, peer], dst.at[w, z], ss.at[w, peer], rs.at[w, z], along_z(peer)).start()
            return 0

        lax.fori_loop(0, nz - 1, go, 0)
        dst[w, z] = src[w, z]

    def z_wait(src, dst, ss, rs, w):
        def go(k, _):
            peer = (z + 1 + k) % nz
            remote(src.at[w, peer], dst.at[w, peer], ss.at[w, peer], rs.at[w, peer],
                   along_z(peer)).wait_recv()
            return 0

        lax.fori_loop(0, nz - 1, go, 0)

    for w in range(2):
        plane_wait(r1, g1, s1, w)
        combine(w)
        z_send(zs, r2, s2, g2, w)

    scores_t = dot(b_proj, c_proj, 1, 1)
    causal_t = iota((tokens, tokens), 0) <= iota((tokens, tokens), 1)
    strict_t = iota((tokens, tokens), 0) < iota((tokens, tokens), 1)
    strict_scores = jnp.where(strict_t, scores_t, 0.0)
    lane = iota((tokens, heads), 1)
    drow[...] = jnp.zeros_like(drow)

    def local_pairs(lo, hi, dscore, dcol):
        for j in range(lo, hi):
            lanes = slice(128 * j, 128 * j + 128)
            grads = out_grad[:, lanes]
            zero = jnp.zeros_like(grads)
            split = jnp.concatenate(
                [jnp.where(first_half, grads, zero), jnp.where(first_half, zero, grads)], axis=0
            )
            products = dot(values[:, lanes], split, 1, 1)
            mixes = []
            for i in range(2):
                h = 2 * j + i
                gap = run_t[h:h + 1, :] - run[:, h:h + 1]
                fall = jnp.exp(jnp.where(causal_t, gap, -1e30))
                mixes.append((fall * scores_t).astype(BF16))
                part = fall * (products[:, 128 * i:128 * i + 128] * dt[:, h:h + 1])
                dscore = dscore + part
                part = part * strict_scores
                drow[h:h + 1, :] = jnp.sum(part, axis=0, keepdims=True)
                dcol = jnp.where(lane == h, jnp.sum(part, axis=1, keepdims=True), dcol)
            dx[:, lanes] = dot(jnp.concatenate(mixes, axis=1), split, 1, 0)
        return dscore, dcol

    dscore = jnp.zeros((tokens, tokens), F32)
    dcol = jnp.zeros((tokens, heads), F32)
    dscore, dcol = local_pairs(0, pairs // 2, dscore, dcol)

    z_decays = None

    def owner_scan(w):
        carry = jnp.zeros((rows, 128), F32)
        for k in range(nz):
            m = k if w == 0 else nz - 1 - k
            bk[w, m] = carry.astype(BF16)
            carry = carry * jnp.exp(zd[m]) + r2[w, m].astype(F32)

    def decay_wait(k, _):
        peer = (z + 1 + k) % nz
        remote(zl.at[peer % 2], zd.at[peer], zl_s.at[peer], zl_r.at[peer], along_z(peer)).wait_recv()
        return 0

    lax.fori_loop(0, nz - 1, decay_wait, 0)
    for w in range(2):
        z_wait(zs, r2, s2, g2, w)
        owner_scan(w)
        z_send(bk, r4, s4, g4, w)

    dscore, dcol = local_pairs(pairs // 2, pairs, dscore, dcol)
    dscore_t = dscore.astype(BF16)
    dscore_n = dscore.T.astype(BF16)
    grad_b = dot(dscore_t, c_proj, 1, 0)
    grad_c = dot(dscore_n, b_proj, 1, 0)
    dr = drow[...].T[:, :heads] - dcol

    def expand(w):
        order = (0, 1, 2, 3) if w == 0 else (3, 2, 1, 0)
        for j in range(nz):
            span = slice((j // 2) * rows, (j // 2) * rows + rows)
            lanes = slice(128 * (j % 2), 128 * (j % 2) + 128)
            carry = r4[w, j].astype(F32)
            for n, q in enumerate(order):
                p5[w, q, span, lanes] = carry.astype(BF16)
                if n < 3:
                    carry = carry * decays[q][:, lanes] + r1[w, q, span, lanes].astype(F32)

    def back_copy(w, d):
        q = (p + d) % 4
        return remote(p5.at[w, q], r5.at[w, p], s5.at[w, d - 1], g5.at[w, p], in_plane(d))

    for w in range(2):
        z_wait(bk, r4, s4, g4, w)
        expand(w)
        for d in (2, 3, 1):
            back_copy(w, d).start()
        r5[w, p] = p5[w, p]

    group = (iota((256, 128), 0) // 64) == iota((256, 128), 1)
    groups = group.astype(F32)

    def head_sums(wide_rows):
        return dot(wide_rows, groups, 1, 0, EXACT)[:, :4]

    plane_wait(r5, g5, s5, 0)
    gains = []
    for q in range(4):
        lanes = slice(256 * q, 256 * q + 256)
        states = r5[0, q]
        grads = gin[:, lanes]
        gains.append(head_sums(dot(c_proj, states, 1, 0) * grads.astype(F32)))
        grad_c = grad_c + dot(grads, states, 1, 1)
    dr = dr + jnp.concatenate(gains, axis=1)

    plane_wait(r5, g5, s5, 1)
    falls, value_dots, kept = [], [], []
    for q in range(4):
        lanes = slice(256 * q, 256 * q + 256)
        exits = r5[1, q]
        fed = vin[:, lanes]
        reach = dot(b_proj, exits, 1, 0)
        falls.append(head_sums(reach * fed.astype(F32)))
        grad_b = grad_b + dot(fed, exits, 1, 1)
        wide_tail = jnp.concatenate([spread(tail, 2 * q), spread(tail, 2 * q + 1)], axis=1)
        full = dx[:, lanes] + reach * wide_tail
        dx[:, lanes] = full
        kept.append(head_sums(jnp.sum(
            exits.astype(F32) * r5[0, q].astype(F32), axis=0, keepdims=True
        )))
    hb[:, :state] = grad_b.astype(BF16)
    hb[:, state:] = grad_c.astype(BF16)
    for d in (2, 1, 3):
        head_copy(hb, gb, hb_s, hb_r, d).start()

    for q in range(4):
        lanes = slice(256 * q, 256 * q + 256)
        full = dx[:, lanes]
        value_dots.append(head_sums(full * values[:, lanes].astype(F32)))
        wide_dt = jnp.concatenate([spread(dt, 2 * q), spread(dt, 2 * q + 1)], axis=1)
        grad_values[:, lanes] = (full * wide_dt).astype(BF16)
    fall = jnp.concatenate(falls, axis=1)
    dr = dr - fall
    at_end = jnp.sum(fall, axis=0, keepdims=True) + ends * jnp.concatenate(kept, axis=1)
    upper = (iota((tokens, tokens), 0) <= iota((tokens, tokens), 1)).astype(F32)
    dlog = dot(upper, dr, 1, 0, EXACT) + at_end
    grad_dt[...] = (jnp.concatenate(value_dots, axis=1) - rate[...] * dlog) * jax.nn.sigmoid(pre)

    total = hb[...].astype(F32)
    for d in (1, 3, 2):
        head_copy(hb, gb, hb_s, hb_r, d).wait_recv()
        total = total + gb[d - 1].astype(F32)
    rounded = total.astype(BF16)

    new_row = iota((2 * state, 2 * state), 0)
    inner = 2 * state // (8 * nz)
    old_row = (
        ((new_row // inner) % nz) * (8 * inner)
        + ((new_row // (inner * nz)) % 2) * (4 * inner)
        + (new_row // (4 * inner * nz)) * (2 * inner)
        + ((new_row // (2 * inner * nz)) % 2) * inner
        + new_row % inner
    )
    pick = (iota((2 * state, 2 * state), 1) == old_row).astype(BF16)
    pt[...] = dot(pick, rounded, 1, 1).astype(BF16)
    there = pt[pl.ds(pl.multiple_of((1 - core) * state, state), state), :]
    here = pt[pl.ds(pl.multiple_of(core * state, state), state), :]

    def pair_copy(c):
        return remote(w0.at[c], e1.at[c], a1.at[c], b1.at[c], other)

    def y_copy(c, d):
        return remote(hs.at[c, d - 1], e2.at[c, d - 1], a2.at[c, d - 1], b2.at[c, d - 1], along_y(d))

    for c in range(2):
        w0[c] = dot(there, features[:, half * c:half * c + half], 1, 0).astype(BF16)
        pair_copy(c).start()
    for c in range(2):
        w1[c] = dot(here, features[:, half * c:half * c + half], 1, 0)
    for c in range(2):
        pair_copy(c).wait_recv()
        for d in (2, 1, 3):
            span = pl.ds(pl.multiple_of(((y + d) % 4) * block, block), block)
            hs[c, d - 1] = (w1[c, span, :] + e1[c, span, :].astype(F32)).astype(BF16)
            y_copy(c, d).start()

    grad_features[...] = dot(rounded, weight[...], 1, 1).astype(BF16)

    for c in range(2):
        span = pl.ds(pl.multiple_of(y * block, block), block)
        total = w1[c, span, :] + e1[c, span, :].astype(F32)
        for d in (1, 3, 2):
            y_copy(c, d).wait_recv()
            total = total + e2[c, d - 1].astype(F32)
        for k in range(nz):
            ws[c, k] = total[2 * k:2 * k + 2].astype(BF16)
        z_send(ws, e3, a3, b3, c)
    for c in range(2):
        z_wait(ws, e3, a3, b3, c)
        total = e3[c, 0].astype(F32)
        for k in range(1, nz):
            total = total + e3[c, k].astype(F32)
        grad_weight[:, half * c:half * c + half] = total

    for d in (1, 2, 3):
        q = (p + d) % 4
        head_copy(ha, ga, ha_s, ha_r, d).wait_send()
        head_copy(hb, gb, hb_s, hb_r, d).wait_send()
        remote(lg.at[q], ld.at[p], lg_s.at[d - 1], lg_r.at[p], in_plane(d)).wait_send()
        for w in range(2):
            plane_copy(sg, r1, s1, g1, w, d).wait_send()
            back_copy(w, d).wait_send()
            y_copy(w, d).wait_send()
    for c in range(2):
        pair_copy(c).wait_send()

    def sent(k, _):
        peer = (z + 1 + k) % nz
        where = along_z(peer)
        remote(zl.at[peer % 2], zd.at[z], zl_s.at[peer], zl_r.at[z], where).wait_send()
        for w in range(2):
            remote(zs.at[w, peer], r2.at[w, z], s2.at[w, peer], g2.at[w, z], where).wait_send()
            remote(bk.at[w, peer], r4.at[w, z], s4.at[w, peer], g4.at[w, z], where).wait_send()
            remote(ws.at[w, peer], e3.at[w, z], a3.at[w, peer], b3.at[w, z], where).wait_send()
        return 0

    lax.fori_loop(0, nz - 1, sent, 0)


def per_device(values, dt_raw, dt_bias, decay_rate, features, bc_weight, out_grad):
    nz = lax.axis_size("ctx") // 4
    tokens, heads = dt_raw.shape[1:]
    feats = features.shape[2]
    two_n = bc_weight.shape[1]
    plan = scratch_plan(nz, tokens, heads, feats, two_n)
    outs = pl.pallas_call(
        make_kernel(list(plan)),
        out_shape=(
            jax.ShapeDtypeStruct(values.shape[1:], BF16),
            jax.ShapeDtypeStruct((tokens, heads), F32),
            jax.ShapeDtypeStruct((tokens, feats), BF16),
            jax.ShapeDtypeStruct((2, feats), F32),
        ),
        in_specs=[VMEM] * 7,
        out_specs=(VMEM,) * 4,
        scratch_shapes=list(plan.values()),
        compiler_params=pltpu.CompilerParams(
            collective_id=0, has_side_effects=True, vmem_limit_bytes=48 << 20
        ),
        name="layer_backward",
    )(values[0], dt_raw[0], dt_bias[None], decay_rate[None], features[0], bc_weight, out_grad[0])
    return (outs[0][None], outs[1][None], outs[2][None], outs[3])


def solution(mesh):
    return jax.shard_map(
        per_device,
        mesh=mesh,
        in_specs=(
            P("dp", "ctx", "head"),
            P("dp", "ctx", "head"),
            P("head"),
            P("head"),
            P("dp", "ctx", "head"),
            P("head", None),
            P("dp", "ctx", "head"),
        ),
        out_specs=(
            P("dp", "ctx", "head"),
            P("dp", "ctx", "head"),
            P("dp", "ctx", "head"),
            P(("ctx", "dp"), "head"),
        ),
        check_vma=False,
    )
```

```python
import jax
import jax.numpy as jnp
from jax import lax
from jax.experimental import pallas as pl
from jax.experimental.pallas import tpu as pltpu
from jax.sharding import PartitionSpec as P

F32 = jnp.float32
BF16 = jnp.bfloat16
EXACT = lax.Precision.HIGHEST
MESH_ID = pl.DeviceIdType.MESH
VMEM = pl.BlockSpec(memory_space=pltpu.VMEM)
HBM = pl.BlockSpec(memory_space=pltpu.HBM)
CHUNKS = 4
DMA = pltpu.SemaphoreType.DMA


def remote(src, dst, send_sem, recv_sem, where):
    return pltpu.make_async_remote_copy(
        src_ref=src, dst_ref=dst, send_sem=send_sem, recv_sem=recv_sem,
        device_id=where, device_id_type=MESH_ID,
    )


def greet(barrier, where):
    pl.semaphore_signal(barrier, inc=1, device_id=where, device_id_type=MESH_ID)


def far_first(k, nz):
    return nz // 2 + (1 - 2 * (k % 2)) * ((k + 1) // 2)


def dot(a, b, ca, cb, precision=None):
    return lax.dot_general(
        a, b, (((ca,), (cb,)), ((), ())), precision=precision, preferred_element_type=F32
    )


def iota(shape, dim):
    return lax.broadcasted_iota(jnp.int32, shape, dim)


def scratch_plan(nz, tokens, heads, feats, two_n):
    rows = 128 // nz
    part = feats // CHUNKS
    block = two_n // 8
    wide = heads * 64
    return dict(
        values=pltpu.VMEM((tokens, wide), BF16),
        raw_t=pltpu.VMEM((heads, tokens), F32),
        bias=pltpu.VMEM((1, heads), F32),
        rate=pltpu.VMEM((1, heads), F32),
        features=pltpu.VMEM((tokens, feats), BF16),
        weight=pltpu.VMEM((feats, two_n), BF16),
        out_grad=pltpu.VMEM((tokens, wide), BF16),
        fetched=DMA((7,)),
        ha=pltpu.VMEM((2, tokens, two_n // 2), BF16),
        hb=pltpu.VMEM((2, tokens, two_n // 2), BF16),
        ga=pltpu.VMEM((2, 3, tokens, two_n // 2), BF16),
        gb=pltpu.VMEM((2, 3, tokens, two_n // 2), BF16),
        ha_s=DMA((2, 3)), ha_r=DMA((2, 3)), hb_s=DMA((2, 3)), hb_r=DMA((2, 3)),
        lg=pltpu.VMEM((4, 1, 256), F32),
        ld=pltpu.VMEM((4, 1, 256), F32),
        zl=pltpu.VMEM((2, 1, 128), F32),
        zd=pltpu.VMEM((nz, 2, 1, 128), F32),
        lg_s=DMA((3,)), lg_r=DMA((4,)), zl_s=DMA((nz,)), zl_r=DMA((nz,)),
        vin=pltpu.VMEM((tokens, wide), BF16),
        gin=pltpu.VMEM((tokens, wide), BF16),
        sg=pltpu.VMEM((2, 128, wide), BF16),
        r1=pltpu.VMEM((4, 4, 128, 128), BF16),
        zs=pltpu.VMEM((4, nz, rows, 128), BF16),
        r2=pltpu.VMEM((4, nz, rows, 128), BF16),
        bk=pltpu.VMEM((4, nz, rows, 128), BF16),
        r4=pltpu.VMEM((4, nz, rows, 128), BF16),
        p5=pltpu.VMEM((4, 4, 128, 128), BF16),
        r5=pltpu.VMEM((4, 4, 128, 128), BF16),
        s1=DMA((4, 3)), g1=DMA((4, 4)), s2=DMA((4, nz)), g2=DMA((4, nz)),
        s4=DMA((4, nz)), g4=DMA((4, nz)), s5=DMA((4, 3)), g5=DMA((4, 4)),
        dx=pltpu.VMEM((tokens, wide), F32),
        drow=pltpu.VMEM((tokens, tokens), F32),
        pt=pltpu.VMEM((two_n, tokens), BF16),
        w0=pltpu.VMEM((CHUNKS, two_n // 2, part), BF16),
        w1=pltpu.VMEM((CHUNKS, two_n // 2, part), F32),
        e1=pltpu.VMEM((CHUNKS, two_n // 2, part), BF16),
        hs=pltpu.VMEM((CHUNKS, 3, block, part), BF16),
        e2=pltpu.VMEM((CHUNKS, 3, block, part), BF16),
        ws=pltpu.VMEM((CHUNKS, nz, 2, part), BF16),
        e3=pltpu.VMEM((CHUNKS, nz, 2, part), BF16),
        a1=DMA((CHUNKS,)), b1=DMA((CHUNKS,)), a2=DMA((CHUNKS, 3)), b2=DMA((CHUNKS, 3)),
        a3=DMA((CHUNKS, nz)), b3=DMA((CHUNKS, nz)),
    )


def make_kernel(names):
    def kernel(*refs):
        step(refs[:7], refs[7:11], **dict(zip(names, refs[11:])))
    return kernel


def step(held, results, *,
         values, raw_t, bias, rate, features, weight, out_grad, fetched,
         ha, hb, ga, gb, ha_s, ha_r, hb_s, hb_r,
         lg, ld, zl, zd, lg_s, lg_r, zl_s, zl_r,
         vin, gin, sg, r1, zs, r2, bk, r4, p5, r5, s1, g1, s2, g2, s4, g4, s5, g5,
         dx, drow, pt, w0, w1, e1, hs, e2, ws, e3, a1, b1, a2, b2, a3, b3):
    grad_values, grad_dt, grad_features, grad_weight = results
    here = (values, raw_t, bias, rate, features, weight, out_grad)
    fetches = [
        pltpu.make_async_copy(held[i], here[i], fetched.at[i]) for i in range(7)
    ]
    for i in (5, 4, 1, 2, 3, 0, 6):
        fetches[i].start()
    ctx, head, dp = lax.axis_index("ctx"), lax.axis_index("head"), lax.axis_index("dp")
    nz = zd.shape[0]
    z, p = ctx // 4, ctx % 4
    low, core = (ctx // 2) % 2, ctx % 2
    y = dp * 2 + low
    rows = 128 // nz
    heads, tokens = raw_t.shape
    pairs = heads // 2
    state = 128
    part = features.shape[1] // CHUNKS
    block = weight.shape[1] // 8

    def at_head(d):
        return {"head": (head + d) % 4}

    def in_plane(d):
        return {"ctx": z * 4 + (p + d) % 4}

    def along_z(peer):
        return {"ctx": peer * 4 + p}

    def along_y(d):
        to = (y + d) % 4
        return {"ctx": z * 4 + (to % 2) * 2 + core, "dp": to // 2}

    other = {"ctx": ctx + 1 - 2 * core}

    barrier = pltpu.get_barrier_semaphore()

    def hello(k, _):
        greet(barrier, along_z((z + far_first(k, nz)) % nz))
        return 0

    lax.fori_loop(0, nz - 1, hello, 0)
    for d in (2, 1, 3):
        greet(barrier, along_y(d))
        greet(barrier, at_head(d))
        greet(barrier, in_plane(d))

    fetches[5].wait()
    fetches[4].wait()
    partial = dot(features[...], weight[...], 1, 0).astype(BF16)
    ha[0] = partial[:, :state]
    ha[1] = partial[:, state:]

    for i in (1, 2, 3):
        fetches[i].wait()

    def flip(few):
        return jnp.concatenate([few, jnp.zeros((128 - heads, tokens), F32)], axis=0).T[:, :heads]

    pre = flip(raw_t[...]) + bias[...]
    dt = jax.nn.softplus(pre)
    lower = (iota((tokens, tokens), 0) >= iota((tokens, tokens), 1)).astype(F32)
    run = dot(lower, -dt * rate[...], 1, 0, EXACT)
    last = run[tokens - 1:tokens, :]
    into = jnp.exp(run)
    tail = jnp.exp(last - run)
    ends = jnp.exp(last)
    run_t = jnp.concatenate([run, jnp.zeros((tokens, 128 - heads), F32)], axis=1).T
    first_half = iota((tokens, 128), 1) < 64

    def spread(cols, j):
        return jnp.where(first_half, cols[:, 2 * j:2 * j + 1], cols[:, 2 * j + 1:2 * j + 2])

    row_half = iota((1, 128), 1) < 64
    for j in range(pairs):
        lg[j // 2, :, 128 * (j % 2):128 * (j % 2) + 128] = jnp.where(
            row_half, last[:, 2 * j:2 * j + 1], last[:, 2 * j + 1:2 * j + 2]
        )
    dt_tail = dt * tail
    fetches[0].wait()
    fetches[6].wait()
    for j in range(pairs):
        lanes = slice(128 * j, 128 * j + 128)
        vin[:, lanes] = (values[:, lanes].astype(F32) * spread(dt_tail, j)).astype(BF16)
        gin[:, lanes] = (out_grad[:, lanes].astype(F32) * spread(into, j)).astype(BF16)

    pl.semaphore_wait(barrier, nz - 1 + 9)

    def head_copy(src, dst, ss, rs, i, d):
        return remote(src.at[i], dst.at[i, d - 1], ss.at[i, d - 1], rs.at[i, d - 1], at_head(d))

    def head_total(src, dst, ss, rs, i):
        total = src[i].astype(F32)
        for d in (1, 3, 2):
            head_copy(src, dst, ss, rs, i, d).wait_recv()
            total = total + dst[i, d - 1].astype(F32)
        return total

    for i in range(2):
        for d in (2, 1, 3):
            head_copy(ha, ga, ha_s, ha_r, i, d).start()
    for d in (2, 3, 1):
        q = (p + d) % 4
        remote(lg.at[q], ld.at[p], lg_s.at[d - 1], lg_r.at[p], in_plane(d)).start()
    ld[p] = lg[p]
    for d in (1, 2, 3):
        q = (p + d) % 4
        remote(lg.at[q], ld.at[q], lg_s.at[d - 1], lg_r.at[q], in_plane(d)).wait_recv()
    whole = ld[0] + ld[1] + ld[2] + ld[3]
    zl[0] = whole[:, :128]
    zl[1] = whole[:, 128:]

    def send_decay(k, _):
        peer = (z + far_first(k, nz)) % nz
        remote(zl, zd.at[z], zl_s.at[peer], zl_r.at[z], along_z(peer)).start()
        return 0

    lax.fori_loop(0, nz - 1, send_decay, 0)
    zd[z] = zl[...]

    def plane_copy(w, d):
        q = (p + d) % 4
        lanes = pl.ds(pl.multiple_of(q * 256 + (w % 2) * 128, 128), 128)
        return remote(sg.at[w // 2, :, lanes], r1.at[w, p], s1.at[w, d - 1], g1.at[w, p], in_plane(d))

    halves = []
    for i, fed in ((0, vin), (1, gin)):
        total = head_total(ha, ga, ha_s, ha_r, i)
        halves.append(total.astype(BF16))
        turned = halves[i].astype(F32).T.astype(BF16)
        sg[i] = dot(turned, fed[...], 1, 0).astype(BF16)
        for w in (2 * i, 2 * i + 1):
            for d in (2, 3, 1):
                plane_copy(w, d).start()
            r1[w, p] = sg[i, :, pl.ds(pl.multiple_of(p * 256 + (w % 2) * 128, 128), 128)]
    b_proj, c_proj = halves

    def plane_wait(buf, rs, ss, w):
        for d in (1, 3, 2):
            q = (p + d) % 4
            remote(buf.at[w, q], buf.at[w, q], ss.at[w, d - 1], rs.at[w, q], in_plane(d)).wait_recv()

    decays = [jnp.exp(ld[q]) for q in range(4)]

    def order_of(w):
        return (0, 1, 2, 3) if w < 2 else (3, 2, 1, 0)

    def decay_of(w, q):
        return decays[q][:, 128 * (w % 2):128 * (w % 2) + 128]

    def combine(w):
        order = order_of(w)
        acc = r1[w, order[0]].astype(F32)
        for q in order[1:]:
            acc = acc * decay_of(w, q) + r1[w, q].astype(F32)
        for j in range(nz):
            zs[w, j] = acc[j * rows:j * rows + rows].astype(BF16)

    def z_send(src, dst, ss, rs, w):
        def go(k, _):
            peer = (z + far_first(k, nz)) % nz
            remote(src.at[w, peer], dst.at[w, z], ss.at[w, peer], rs.at[w, z], along_z(peer)).start()
            return 0

        lax.fori_loop(0, nz - 1, go, 0)
        dst[w, z] = src[w, z]

    def z_wait(src, dst, ss, rs, w):
        def go(k, _):
            peer = (z + 1 + k) % nz
            remote(src.at[w, peer], dst.at[w, peer], ss.at[w, peer], rs.at[w, peer],
                   along_z(peer)).wait_recv()
            return 0

        lax.fori_loop(0, nz - 1, go, 0)

    for w in range(4):
        plane_wait(r1, g1, s1, w)
        combine(w)
        z_send(zs, r2, s2, g2, w)

    scores_t = dot(b_proj, c_proj, 1, 1)
    causal_t = iota((tokens, tokens), 0) <= iota((tokens, tokens), 1)
    strict_t = iota((tokens, tokens), 0) < iota((tokens, tokens), 1)
    strict_scores = jnp.where(strict_t, scores_t, 0.0)
    lane = iota((tokens, heads), 1)
    drow[...] = jnp.zeros_like(drow)

    def local_pairs(lo, hi, dscore, dcol):
        for j in range(lo, hi):
            lanes = slice(128 * j, 128 * j + 128)
            grads = out_grad[:, lanes]
            zero = jnp.zeros_like(grads)
            split = jnp.concatenate(
                [jnp.where(first_half, grads, zero), jnp.where(first_half, zero, grads)], axis=0
            )
            products = dot(values[:, lanes], split, 1, 1)
            mixes = []
            for i in range(2):
                h = 2 * j + i
                gap = run_t[h:h + 1, :] - run[:, h:h + 1]
                fall = jnp.exp(jnp.where(causal_t, gap, -1e30))
                mixes.append((fall * scores_t).astype(BF16))
                part = fall * (products[:, 128 * i:128 * i + 128] * dt[:, h:h + 1])
                dscore = dscore + part
                part = part * strict_scores
                drow[h:h + 1, :] = jnp.sum(part, axis=0, keepdims=True)
                dcol = jnp.where(lane == h, jnp.sum(part, axis=1, keepdims=True), dcol)
            dx[:, lanes] = dot(jnp.concatenate(mixes, axis=1), split, 1, 0)
        return dscore, dcol

    dscore = jnp.zeros((tokens, tokens), F32)
    dcol = jnp.zeros((tokens, heads), F32)
    dscore, dcol = local_pairs(0, pairs // 2, dscore, dcol)

    def owner_scan(w):
        carry = jnp.zeros((rows, 128), F32)
        for k in range(nz):
            m = k if w < 2 else nz - 1 - k
            bk[w, m] = carry.astype(BF16)
            carry = carry * jnp.exp(zd[m, w % 2]) + r2[w, m].astype(F32)

    def decay_wait(k, _):
        peer = (z + 1 + k) % nz
        remote(zl, zd.at[peer], zl_s.at[peer], zl_r.at[peer], along_z(peer)).wait_recv()
        return 0

    lax.fori_loop(0, nz - 1, decay_wait, 0)
    for w in range(4):
        z_wait(zs, r2, s2, g2, w)
        owner_scan(w)
        z_send(bk, r4, s4, g4, w)

    dscore, dcol = local_pairs(pairs // 2, pairs, dscore, dcol)
    dscore_t = dscore.astype(BF16)
    dscore_n = dscore.T.astype(BF16)
    grad_b = dot(dscore_t, c_proj, 1, 0)
    grad_c = dot(dscore_n, b_proj, 1, 0)
    dr = drow[...].T[:, :heads] - dcol

    def expand(w):
        for j in range(nz):
            span = slice(j * rows, j * rows + rows)
            carry = r4[w, j].astype(F32)
            for n, q in enumerate(order_of(w)):
                p5[w, q, span, :] = carry.astype(BF16)
                if n < 3:
                    carry = carry * decay_of(w, q) + r1[w, q, span, :].astype(F32)

    def back_copy(w, d):
        q = (p + d) % 4
        return remote(p5.at[w, q], r5.at[w, p], s5.at[w, d - 1], g5.at[w, p], in_plane(d))

    for w in range(4):
        z_wait(bk, r4, s4, g4, w)
        expand(w)
        for d in (2, 3, 1):
            back_copy(w, d).start()
        r5[w, p] = p5[w, p]

    group = (iota((256, 128), 0) // 64) == iota((256, 128), 1)
    groups = group.astype(F32)

    def head_sums(wide_rows):
        return dot(wide_rows, groups, 1, 0, EXACT)[:, :4]

    def entering(i, q):
        return jnp.concatenate([r5[2 * i, q], r5[2 * i + 1, q]], axis=1)

    plane_wait(r5, g5, s5, 0)
    plane_wait(r5, g5, s5, 1)
    for q in range(4):
        grad_c = grad_c + dot(gin[:, 256 * q:256 * q + 256], entering(0, q), 1, 1)
    hb[1] = grad_c.astype(BF16)
    for d in (2, 1, 3):
        head_copy(hb, gb, hb_s, hb_r, 1, d).start()
    gains = []
    for q in range(4):
        lanes = slice(256 * q, 256 * q + 256)
        gains.append(head_sums(dot(c_proj, entering(0, q), 1, 0) * gin[:, lanes].astype(F32)))
    dr = dr + jnp.concatenate(gains, axis=1)

    plane_wait(r5, g5, s5, 2)
    plane_wait(r5, g5, s5, 3)
    for q in range(4):
        grad_b = grad_b + dot(vin[:, 256 * q:256 * q + 256], entering(1, q), 1, 1)
    hb[0] = grad_b.astype(BF16)
    for d in (2, 1, 3):
        head_copy(hb, gb, hb_s, hb_r, 0, d).start()

    falls, value_dots, kept = [], [], []
    for q in range(4):
        lanes = slice(256 * q, 256 * q + 256)
        exits = entering(1, q)
        reach = dot(b_proj, exits, 1, 0)
        falls.append(head_sums(reach * vin[:, lanes].astype(F32)))
        wide_tail = jnp.concatenate([spread(tail, 2 * q), spread(tail, 2 * q + 1)], axis=1)
        full = dx[:, lanes] + reach * wide_tail
        kept.append(head_sums(jnp.sum(
            exits.astype(F32) * entering(0, q).astype(F32), axis=0, keepdims=True
        )))
        value_dots.append(head_sums(full * values[:, lanes].astype(F32)))
        wide_dt = jnp.concatenate([spread(dt, 2 * q), spread(dt, 2 * q + 1)], axis=1)
        grad_values[:, lanes] = (full * wide_dt).astype(BF16)
    fall = jnp.concatenate(falls, axis=1)
    dr = dr - fall
    at_end = jnp.sum(fall, axis=0, keepdims=True) + ends * jnp.concatenate(kept, axis=1)
    upper = (iota((tokens, tokens), 0) <= iota((tokens, tokens), 1)).astype(F32)
    dlog = dot(upper, dr, 1, 0, EXACT) + at_end
    grads = (jnp.concatenate(value_dots, axis=1) - rate[...] * dlog) * jax.nn.sigmoid(pre)
    grad_dt[...] = jnp.concatenate([grads, jnp.zeros((tokens, 128 - heads), F32)], axis=1).T[:heads]

    grad_cs = head_total(hb, gb, hb_s, hb_r, 1).astype(BF16)
    grad_bs = head_total(hb, gb, hb_s, hb_r, 0).astype(BF16)
    rounded = jnp.concatenate([grad_bs, grad_cs], axis=1)

    new_row = iota((2 * state, 2 * state), 0)
    inner = 2 * state // (8 * nz)
    old_row = (
        ((new_row // inner) % nz) * (8 * inner)
        + ((new_row // (inner * nz)) % 2) * (4 * inner)
        + (new_row // (4 * inner * nz)) * (2 * inner)
        + ((new_row // (2 * inner * nz)) % 2) * inner
        + new_row % inner
    )
    pick = (iota((2 * state, 2 * state), 1) == old_row).astype(BF16)
    pt[...] = dot(pick, rounded, 1, 1).astype(BF16)
    theirs = pt[pl.ds(pl.multiple_of((1 - core) * state, state), state), :]
    ours = pt[pl.ds(pl.multiple_of(core * state, state), state), :]

    def pair_copy(c):
        return remote(w0.at[c], e1.at[c], a1.at[c], b1.at[c], other)

    def y_copy(c, d):
        return remote(hs.at[c, d - 1], e2.at[c, d - 1], a2.at[c, d - 1], b2.at[c, d - 1], along_y(d))

    for c in range(CHUNKS):
        w0[c] = dot(theirs, features[:, part * c:part * c + part], 1, 0).astype(BF16)
        pair_copy(c).start()
    for c in range(CHUNKS):
        w1[c] = dot(ours, features[:, part * c:part * c + part], 1, 0)
    for c in range(CHUNKS):
        pair_copy(c).wait_recv()
        for d in (2, 1, 3):
            span = pl.ds(pl.multiple_of(((y + d) % 4) * block, block), block)
            hs[c, d - 1] = (w1[c, span, :] + e1[c, span, :].astype(F32)).astype(BF16)
            y_copy(c, d).start()

    grad_features[...] = dot(rounded, weight[...], 1, 1).astype(BF16)

    for c in range(CHUNKS):
        span = pl.ds(pl.multiple_of(y * block, block), block)
        total = w1[c, span, :] + e1[c, span, :].astype(F32)
        for d in (1, 3, 2):
            y_copy(c, d).wait_recv()
            total = total + e2[c, d - 1].astype(F32)
        for k in range(nz):
            ws[c, k] = total[2 * k:2 * k + 2].astype(BF16)
        z_send(ws, e3, a3, b3, c)
    for c in range(CHUNKS):
        z_wait(ws, e3, a3, b3, c)
        total = e3[c, 0].astype(F32)
        for k in range(1, nz):
            total = total + e3[c, k].astype(F32)
        grad_weight[:, part * c:part * c + part] = total

    for d in (1, 2, 3):
        q = (p + d) % 4
        for i in range(2):
            head_copy(ha, ga, ha_s, ha_r, i, d).wait_send()
            head_copy(hb, gb, hb_s, hb_r, i, d).wait_send()
        remote(lg.at[q], ld.at[p], lg_s.at[d - 1], lg_r.at[p], in_plane(d)).wait_send()
        for w in range(4):
            plane_copy(w, d).wait_send()
            back_copy(w, d).wait_send()
        for c in range(CHUNKS):
            y_copy(c, d).wait_send()
    for c in range(CHUNKS):
        pair_copy(c).wait_send()

    def sent(k, _):
        peer = (z + 1 + k) % nz
        where = along_z(peer)
        remote(zl, zd.at[z], zl_s.at[peer], zl_r.at[z], where).wait_send()
        for w in range(4):
            remote(zs.at[w, peer], r2.at[w, z], s2.at[w, peer], g2.at[w, z], where).wait_send()
            remote(bk.at[w, peer], r4.at[w, z], s4.at[w, peer], g4.at[w, z], where).wait_send()
        for c in range(CHUNKS):
            remote(ws.at[c, peer], e3.at[c, z], a3.at[c, peer], b3.at[c, z], where).wait_send()
        return 0

    lax.fori_loop(0, nz - 1, sent, 0)


def deliver_kernel(*refs):
    sems = refs[8]
    copies = [pltpu.make_async_copy(refs[i], refs[4 + i], sems.at[i]) for i in range(4)]
    for copy in copies:
        copy.start()
    for copy in copies:
        copy.wait()


def deliver(outs):
    return pl.pallas_call(
        deliver_kernel,
        out_shape=tuple(jax.ShapeDtypeStruct(o.shape, o.dtype) for o in outs),
        in_specs=[VMEM] * 4,
        out_specs=(HBM,) * 4,
        scratch_shapes=[DMA((4,))],
        compiler_params=pltpu.CompilerParams(vmem_limit_bytes=8 << 20),
        name="deliver",
    )(*outs)


def per_device(values, dt_raw, dt_bias, decay_rate, features, bc_weight, out_grad):
    nz = lax.axis_size("ctx") // 4
    tokens, heads = dt_raw.shape[1:]
    feats = features.shape[2]
    two_n = bc_weight.shape[1]
    plan = scratch_plan(nz, tokens, heads, feats, two_n)
    outs = pl.pallas_call(
        make_kernel(list(plan)),
        out_shape=(
            jax.ShapeDtypeStruct(values.shape[1:], BF16),
            jax.ShapeDtypeStruct((heads, tokens), F32),
            jax.ShapeDtypeStruct((tokens, feats), BF16),
            jax.ShapeDtypeStruct((2, feats), F32),
        ),
        in_specs=[HBM] * 7,
        out_specs=(VMEM,) * 4,
        scratch_shapes=list(plan.values()),
        compiler_params=pltpu.CompilerParams(
            collective_id=0, has_side_effects=True, vmem_limit_bytes=48 << 20
        ),
        name="layer_backward",
    )(*[pltpu.with_memory_space_constraint(x, pltpu.HBM) for x in (
        values[0], dt_raw[0].T, dt_bias[None], decay_rate[None], features[0], bc_weight, out_grad[0]
    )])
    outs = deliver(outs)
    return (outs[0][None], outs[1].T[None], outs[2][None], outs[3])


def solution(mesh):
    return jax.shard_map(
        per_device,
        mesh=mesh,
        in_specs=(
            P("dp", "ctx", "head"),
            P("dp", "ctx", "head"),
            P("head"),
            P("head"),
            P("dp", "ctx", "head"),
            P("head", None),
            P("dp", "ctx", "head"),
        ),
        out_specs=(
            P("dp", "ctx", "head"),
            P("dp", "ctx", "head"),
            P("dp", "ctx", "head"),
            P(("ctx", "dp"), "head"),
        ),
        check_vma=False,
    )
```

```python
import jax
import jax.numpy as jnp
from jax import lax
from jax.experimental import pallas as pl
from jax.experimental.pallas import tpu as pltpu
from jax.sharding import PartitionSpec as P

F32 = jnp.float32
BF16 = jnp.bfloat16
EXACT = lax.Precision.HIGHEST
MESH_ID = pl.DeviceIdType.MESH
VMEM = pl.BlockSpec(memory_space=pltpu.VMEM)
HBM = pl.BlockSpec(memory_space=pltpu.HBM)
CHUNKS = 4
DMA = pltpu.SemaphoreType.DMA


def remote(src, dst, send_sem, recv_sem, where):
    return pltpu.make_async_remote_copy(
        src_ref=src, dst_ref=dst, send_sem=send_sem, recv_sem=recv_sem,
        device_id=where, device_id_type=MESH_ID,
    )


def greet(barrier, where):
    pl.semaphore_signal(barrier, inc=1, device_id=where, device_id_type=MESH_ID)


def far_first(k, nz):
    return nz // 2 + (1 - 2 * (k % 2)) * ((k + 1) // 2)


def dot(a, b, ca, cb, precision=None):
    return lax.dot_general(
        a, b, (((ca,), (cb,)), ((), ())), precision=precision, preferred_element_type=F32
    )


def iota(shape, dim):
    return lax.broadcasted_iota(jnp.int32, shape, dim)


def scratch_plan(nz, tokens, heads, feats, two_n):
    rows = 128 // nz
    part = feats // CHUNKS
    block = two_n // 8
    wide = heads * 64
    return dict(
        values=pltpu.VMEM((tokens, wide), BF16),
        raw_t=pltpu.VMEM((heads, tokens), F32),
        bias=pltpu.VMEM((1, heads), F32),
        rate=pltpu.VMEM((1, heads), F32),
        features=pltpu.VMEM((2, tokens, feats), BF16),
        weight=pltpu.VMEM((feats, two_n), BF16),
        out_grad=pltpu.VMEM((tokens, wide), BF16),
        fetched=DMA((7,)),
        relay=pltpu.SemaphoreType.REGULAR((max(nz.bit_length() - 2, 1),)),
        ha=pltpu.VMEM((2, tokens, two_n // 2), BF16),
        hb=pltpu.VMEM((2, tokens, two_n // 2), BF16),
        ga=pltpu.VMEM((2, 3, tokens, two_n // 2), BF16),
        gb=pltpu.VMEM((2, 3, tokens, two_n // 2), BF16),
        ha_s=DMA((2, 3)), ha_r=DMA((2, 3)), hb_s=DMA((2, 3)), hb_r=DMA((2, 3)),
        lg=pltpu.VMEM((4, 1, 256), F32),
        ld=pltpu.VMEM((4, 1, 256), F32),
        zl=pltpu.VMEM((2, 1, 128), F32),
        zd=pltpu.VMEM((nz, 2, 1, 128), F32),
        lg_s=DMA((3,)), lg_r=DMA((4,)), zl_s=DMA((nz,)), zl_r=DMA((nz,)),
        vin=pltpu.VMEM((tokens, wide), BF16),
        gin=pltpu.VMEM((tokens, wide), BF16),
        sg=pltpu.VMEM((2, 128, wide), BF16),
        r1=pltpu.VMEM((4, 4, 128, 128), BF16),
        zs=pltpu.VMEM((4, nz, rows, 128), BF16),
        r2=pltpu.VMEM((4, nz, rows, 128), BF16),
        bk=pltpu.VMEM((4, nz, rows, 128), BF16),
        r4=pltpu.VMEM((4, nz, rows, 128), BF16),
        p5=pltpu.VMEM((4, 4, 128, 128), BF16),
        r5=pltpu.VMEM((4, 4, 128, 128), BF16),
        s1=DMA((4, 3)), g1=DMA((4, 4)), s2=DMA((4, nz)), g2=DMA((4, nz)),
        s4=DMA((4, nz)), g4=DMA((4, nz)), s5=DMA((4, 3)), g5=DMA((4, 4)),
        dx=pltpu.VMEM((tokens, wide), F32),
        drow=pltpu.VMEM((tokens, tokens), F32),
        pt=pltpu.VMEM((two_n, tokens), BF16),
        w1=pltpu.VMEM((CHUNKS, two_n // 2, part), F32),
        e1=pltpu.VMEM((two_n // 2, tokens), BF16),
        hs=pltpu.VMEM((CHUNKS, 3, block, part), BF16),
        e2=pltpu.VMEM((CHUNKS, 3, block, part), BF16),
        ws=pltpu.VMEM((CHUNKS, nz, 2, part), BF16),
        e3=pltpu.VMEM((CHUNKS, nz, 2, part), BF16),
        f_s=DMA((1,)), f_r=DMA((1,)), a1=DMA((1,)), b1=DMA((1,)), a2=DMA((CHUNKS, 3)), b2=DMA((CHUNKS, 3)),
        a3=DMA((CHUNKS, nz)), b3=DMA((CHUNKS, nz)),
    )


def make_kernel(names):
    def kernel(*refs):
        step(refs[:7], refs[7:11], **dict(zip(names, refs[11:])))
    return kernel


def step(held, results, *,
         values, raw_t, bias, rate, features, weight, out_grad, fetched, relay,
         ha, hb, ga, gb, ha_s, ha_r, hb_s, hb_r,
         lg, ld, zl, zd, lg_s, lg_r, zl_s, zl_r,
         vin, gin, sg, r1, zs, r2, bk, r4, p5, r5, s1, g1, s2, g2, s4, g4, s5, g5,
         dx, drow, pt, w1, e1, hs, e2, ws, e3, f_s, f_r, a1, b1, a2, b2, a3, b3):
    grad_values, grad_dt, grad_features, grad_weight = results
    here = (values, raw_t, bias, rate, features.at[0], weight, out_grad)
    fetches = [
        pltpu.make_async_copy(held[i], here[i], fetched.at[i]) for i in range(7)
    ]
    for i in (5, 4, 1, 2, 3, 0, 6):
        fetches[i].start()
    ctx, head, dp = lax.axis_index("ctx"), lax.axis_index("head"), lax.axis_index("dp")
    nz = zd.shape[0]
    z, p = ctx // 4, ctx % 4
    low, core = (ctx // 2) % 2, ctx % 2
    y = dp * 2 + low
    rows = 128 // nz
    heads, tokens = raw_t.shape
    pairs = heads // 2
    state = 128
    part = features.shape[2] // CHUNKS
    block = weight.shape[1] // 8

    def at_head(d):
        return {"head": (head + d) % 4}

    def in_plane(d):
        return {"ctx": z * 4 + (p + d) % 4}

    def along_z(peer):
        return {"ctx": peer * 4 + p}

    def along_y(d):
        to = (y + d) % 4
        return {"ctx": z * 4 + (to % 2) * 2 + core, "dp": to // 2}

    other = {"ctx": ctx + 1 - 2 * core}

    barrier = pltpu.get_barrier_semaphore()
    for d in (2, 1, 3):
        greet(barrier, at_head(d))
    for d in (1, nz - 1):
        greet(barrier, along_z((z + d) % nz))
    for d in (2, 1, 3):
        greet(barrier, along_y(d))
        greet(barrier, in_plane(d))

    fetches[5].wait()
    fetches[4].wait()
    partial = dot(features[0], weight[...], 1, 0).astype(BF16)
    ha[0] = partial[:, :state]
    ha[1] = partial[:, state:]

    pl.semaphore_wait(barrier, 11)

    reaches = [1 << i for i in range(nz.bit_length() - 2)]

    def relay_signal(i):
        for d in (reaches[i], nz - reaches[i]):
            pl.semaphore_signal(
                relay.at[i], inc=1, device_id=along_z((z + d) % nz), device_id_type=MESH_ID
            )

    def relay_wait(i):
        pl.semaphore_wait(relay.at[i], 2)

    def head_copy(src, dst, ss, rs, i, d):
        return remote(src.at[i], dst.at[i, d - 1], ss.at[i, d - 1], rs.at[i, d - 1], at_head(d))

    def head_total(src, dst, ss, rs, i):
        total = src[i].astype(F32)
        for d in (1, 3, 2):
            head_copy(src, dst, ss, rs, i, d).wait_recv()
            total = total + dst[i, d - 1].astype(F32)
        return total

    for i in range(2):
        for d in (2, 1, 3):
            head_copy(ha, ga, ha_s, ha_r, i, d).start()
    relay_signal(0)

    for i in (1, 2, 3):
        fetches[i].wait()

    def flip(few):
        return jnp.concatenate([few, jnp.zeros((128 - heads, tokens), F32)], axis=0).T[:, :heads]

    pre = flip(raw_t[...]) + bias[...]
    dt = jax.nn.softplus(pre)
    lower = (iota((tokens, tokens), 0) >= iota((tokens, tokens), 1)).astype(F32)
    run = dot(lower, -dt * rate[...], 1, 0, EXACT)
    last = run[tokens - 1:tokens, :]
    into = jnp.exp(run)
    tail = jnp.exp(last - run)
    ends = jnp.exp(last)
    run_t = jnp.concatenate([run, jnp.zeros((tokens, 128 - heads), F32)], axis=1).T
    first_half = iota((tokens, 128), 1) < 64

    def spread(cols, j):
        return jnp.where(first_half, cols[:, 2 * j:2 * j + 1], cols[:, 2 * j + 1:2 * j + 2])

    row_half = iota((1, 128), 1) < 64
    for j in range(pairs):
        lg[j // 2, :, 128 * (j % 2):128 * (j % 2) + 128] = jnp.where(
            row_half, last[:, 2 * j:2 * j + 1], last[:, 2 * j + 1:2 * j + 2]
        )
    dt_tail = dt * tail
    fetches[0].wait()
    fetches[6].wait()
    for j in range(pairs):
        lanes = slice(128 * j, 128 * j + 128)
        vin[:, lanes] = (values[:, lanes].astype(F32) * spread(dt_tail, j)).astype(BF16)
        gin[:, lanes] = (out_grad[:, lanes].astype(F32) * spread(into, j)).astype(BF16)

    for d in (2, 3, 1):
        q = (p + d) % 4
        remote(lg.at[q], ld.at[p], lg_s.at[d - 1], lg_r.at[p], in_plane(d)).start()
    for i in range(len(reaches) - 1):
        relay_wait(i)
        relay_signal(i + 1)

    def plane_copy(w, d):
        q = (p + d) % 4
        lanes = pl.ds(pl.multiple_of(q * 256 + (w % 2) * 128, 128), 128)
        return remote(sg.at[w // 2, :, lanes], r1.at[w, p], s1.at[w, d - 1], g1.at[w, p], in_plane(d))

    halves = []
    for i, fed in ((0, vin), (1, gin)):
        total = head_total(ha, ga, ha_s, ha_r, i)
        halves.append(total.astype(BF16))
        turned = halves[i].astype(F32).T.astype(BF16)
        sg[i] = dot(turned, fed[...], 1, 0).astype(BF16)
        for w in (2 * i, 2 * i + 1):
            for d in (2, 3, 1):
                plane_copy(w, d).start()
            r1[w, p] = sg[i, :, pl.ds(pl.multiple_of(p * 256 + (w % 2) * 128, 128), 128)]
    b_proj, c_proj = halves

    def plane_wait(buf, rs, ss, w):
        for d in (1, 3, 2):
            q = (p + d) % 4
            remote(buf.at[w, q], buf.at[w, q], ss.at[w, d - 1], rs.at[w, q], in_plane(d)).wait_recv()

    def order_of(w):
        return (0, 1, 2, 3) if w < 2 else (3, 2, 1, 0)

    def decay_of(w, q):
        return decays[q][:, 128 * (w % 2):128 * (w % 2) + 128]

    def combine(w):
        order = order_of(w)
        acc = r1[w, order[0]].astype(F32)
        for q in order[1:]:
            acc = acc * decay_of(w, q) + r1[w, q].astype(F32)
        for j in range(nz):
            zs[w, j] = acc[j * rows:j * rows + rows].astype(BF16)

    def z_send(src, dst, ss, rs, w):
        def go(k, _):
            peer = (z + far_first(k, nz)) % nz
            remote(src.at[w, peer], dst.at[w, z], ss.at[w, peer], rs.at[w, z], along_z(peer)).start()
            return 0

        lax.fori_loop(0, nz - 1, go, 0)
        dst[w, z] = src[w, z]

    def z_wait(src, dst, ss, rs, w):
        def go(k, _):
            peer = (z + 1 + k) % nz
            remote(src.at[w, peer], dst.at[w, peer], ss.at[w, peer], rs.at[w, peer],
                   along_z(peer)).wait_recv()
            return 0

        lax.fori_loop(0, nz - 1, go, 0)

    ld[p] = lg[p]
    for d in (1, 2, 3):
        q = (p + d) % 4
        remote(lg.at[q], ld.at[q], lg_s.at[d - 1], lg_r.at[q], in_plane(d)).wait_recv()
    whole = ld[0] + ld[1] + ld[2] + ld[3]
    zl[0] = whole[:, :128]
    zl[1] = whole[:, 128:]

    relay_wait(len(reaches) - 1)

    decays = [jnp.exp(ld[q]) for q in range(4)]

    def send_decay(k, _):
        peer = (z + far_first(k, nz)) % nz
        remote(zl, zd.at[z], zl_s.at[peer], zl_r.at[z], along_z(peer)).start()
        return 0

    lax.fori_loop(0, nz - 1, send_decay, 0)
    zd[z] = zl[...]

    for w in range(4):
        plane_wait(r1, g1, s1, w)
        combine(w)
        z_send(zs, r2, s2, g2, w)

    feature_copy = remote(features.at[0], features.at[1], f_s.at[0], f_r.at[0], other)
    feature_copy.start()

    scores_t = dot(b_proj, c_proj, 1, 1)
    causal_t = iota((tokens, tokens), 0) <= iota((tokens, tokens), 1)
    strict_t = iota((tokens, tokens), 0) < iota((tokens, tokens), 1)
    strict_scores = jnp.where(strict_t, scores_t, 0.0)
    lane = iota((tokens, heads), 1)
    drow[...] = jnp.zeros_like(drow)

    def local_pairs(lo, hi, dscore, dcol):
        for j in range(lo, hi):
            lanes = slice(128 * j, 128 * j + 128)
            grads = out_grad[:, lanes]
            zero = jnp.zeros_like(grads)
            split = jnp.concatenate(
                [jnp.where(first_half, grads, zero), jnp.where(first_half, zero, grads)], axis=0
            )
            products = dot(values[:, lanes], split, 1, 1)
            mixes = []
            for i in range(2):
                h = 2 * j + i
                gap = run_t[h:h + 1, :] - run[:, h:h + 1]
                fall = jnp.exp(jnp.where(causal_t, gap, -1e30))
                mixes.append((fall * scores_t).astype(BF16))
                part = fall * (products[:, 128 * i:128 * i + 128] * dt[:, h:h + 1])
                dscore = dscore + part
                part = part * strict_scores
                drow[h:h + 1, :] = jnp.sum(part, axis=0, keepdims=True)
                dcol = jnp.where(lane == h, jnp.sum(part, axis=1, keepdims=True), dcol)
            dx[:, lanes] = dot(jnp.concatenate(mixes, axis=1), split, 1, 0)
        return dscore, dcol

    dscore = jnp.zeros((tokens, tokens), F32)
    dcol = jnp.zeros((tokens, heads), F32)
    dscore, dcol = local_pairs(0, pairs // 2, dscore, dcol)

    def owner_scan(w):
        carry = jnp.zeros((rows, 128), F32)
        for k in range(nz):
            m = k if w < 2 else nz - 1 - k
            bk[w, m] = carry.astype(BF16)
            carry = carry * jnp.exp(zd[m, w % 2]) + r2[w, m].astype(F32)

    def decay_wait(k, _):
        peer = (z + 1 + k) % nz
        remote(zl, zd.at[peer], zl_s.at[peer], zl_r.at[peer], along_z(peer)).wait_recv()
        return 0

    lax.fori_loop(0, nz - 1, decay_wait, 0)
    for w in range(4):
        z_wait(zs, r2, s2, g2, w)
        owner_scan(w)
        z_send(bk, r4, s4, g4, w)

    dscore, dcol = local_pairs(pairs // 2, pairs, dscore, dcol)
    dscore_t = dscore.astype(BF16)
    dscore_n = dscore.T.astype(BF16)
    grad_b = dot(dscore_t, c_proj, 1, 0)
    grad_c = dot(dscore_n, b_proj, 1, 0)
    dr = drow[...].T[:, :heads] - dcol

    def expand(w):
        for j in range(nz):
            span = slice(j * rows, j * rows + rows)
            carry = r4[w, j].astype(F32)
            for n, q in enumerate(order_of(w)):
                p5[w, q, span, :] = carry.astype(BF16)
                if n < 3:
                    carry = carry * decay_of(w, q) + r1[w, q, span, :].astype(F32)

    def back_copy(w, d):
        q = (p + d) % 4
        return remote(p5.at[w, q], r5.at[w, p], s5.at[w, d - 1], g5.at[w, p], in_plane(d))

    for w in range(4):
        z_wait(bk, r4, s4, g4, w)
        expand(w)
        for d in (2, 3, 1):
            back_copy(w, d).start()
        r5[w, p] = p5[w, p]

    group = (iota((256, 128), 0) // 64) == iota((256, 128), 1)
    groups = group.astype(F32)

    def head_sums(wide_rows):
        return dot(wide_rows, groups, 1, 0, EXACT)[:, :4]

    def entering(i, q):
        return jnp.concatenate([r5[2 * i, q], r5[2 * i + 1, q]], axis=1)

    plane_wait(r5, g5, s5, 0)
    plane_wait(r5, g5, s5, 1)
    for q in range(4):
        grad_c = grad_c + dot(gin[:, 256 * q:256 * q + 256], entering(0, q), 1, 1)
    hb[1] = grad_c.astype(BF16)
    for d in (2, 1, 3):
        head_copy(hb, gb, hb_s, hb_r, 1, d).start()
    plane_wait(r5, g5, s5, 2)
    plane_wait(r5, g5, s5, 3)
    for q in range(4):
        grad_b = grad_b + dot(vin[:, 256 * q:256 * q + 256], entering(1, q), 1, 1)
    hb[0] = grad_b.astype(BF16)
    for d in (2, 1, 3):
        head_copy(hb, gb, hb_s, hb_r, 0, d).start()

    grad_cs = head_total(hb, gb, hb_s, hb_r, 1).astype(BF16)
    grad_bs = head_total(hb, gb, hb_s, hb_r, 0).astype(BF16)
    rounded = jnp.concatenate([grad_bs, grad_cs], axis=1)

    new_row = iota((2 * state, 2 * state), 0)
    inner = 2 * state // (8 * nz)
    old_row = (
        ((new_row // inner) % nz) * (8 * inner)
        + ((new_row // (inner * nz)) % 2) * (4 * inner)
        + (new_row // (4 * inner * nz)) * (2 * inner)
        + ((new_row // (2 * inner * nz)) % 2) * inner
        + new_row % inner
    )
    pick = (iota((2 * state, 2 * state), 1) == old_row).astype(BF16)
    pt[...] = dot(pick, rounded, 1, 1).astype(BF16)
    ours = pt[pl.ds(pl.multiple_of(core * state, state), state), :]
    pair_copy = remote(
        pt.at[pl.ds(pl.multiple_of((1 - core) * state, state), state)],
        e1, a1.at[0], b1.at[0], other,
    )
    pair_copy.start()

    def y_copy(c, d):
        return remote(hs.at[c, d - 1], e2.at[c, d - 1], a2.at[c, d - 1], b2.at[c, d - 1], along_y(d))

    feature_copy.wait_recv()
    pair_copy.wait_recv()
    both = jnp.concatenate([ours, e1[...]], axis=1)
    for c in range(CHUNKS):
        lanes = slice(part * c, part * c + part)
        fed = jnp.concatenate([features[0, :, lanes], features[1, :, lanes]], axis=0)
        w1[c] = dot(both, fed, 1, 0)
        for d in (2, 1, 3):
            span = pl.ds(pl.multiple_of(((y + d) % 4) * block, block), block)
            hs[c, d - 1] = w1[c, span, :].astype(BF16)
            y_copy(c, d).start()

    grad_features[...] = dot(rounded, weight[...], 1, 1).astype(BF16)

    for c in range(CHUNKS):
        span = pl.ds(pl.multiple_of(y * block, block), block)
        total = w1[c, span, :]
        for d in (1, 3, 2):
            y_copy(c, d).wait_recv()
            total = total + e2[c, d - 1].astype(F32)
        for k in range(nz):
            ws[c, k] = total[2 * k:2 * k + 2].astype(BF16)
        z_send(ws, e3, a3, b3, c)
    gains = []
    for q in range(4):
        lanes = slice(256 * q, 256 * q + 256)
        gains.append(head_sums(dot(c_proj, entering(0, q), 1, 0) * gin[:, lanes].astype(F32)))
    dr = dr + jnp.concatenate(gains, axis=1)

    falls, value_dots, kept = [], [], []
    for q in range(4):
        lanes = slice(256 * q, 256 * q + 256)
        exits = entering(1, q)
        reach = dot(b_proj, exits, 1, 0)
        falls.append(head_sums(reach * vin[:, lanes].astype(F32)))
        wide_tail = jnp.concatenate([spread(tail, 2 * q), spread(tail, 2 * q + 1)], axis=1)
        full = dx[:, lanes] + reach * wide_tail
        kept.append(head_sums(jnp.sum(
            exits.astype(F32) * entering(0, q).astype(F32), axis=0, keepdims=True
        )))
        value_dots.append(head_sums(full * values[:, lanes].astype(F32)))
        wide_dt = jnp.concatenate([spread(dt, 2 * q), spread(dt, 2 * q + 1)], axis=1)
        grad_values[:, lanes] = (full * wide_dt).astype(BF16)
    fall = jnp.concatenate(falls, axis=1)
    dr = dr - fall
    at_end = jnp.sum(fall, axis=0, keepdims=True) + ends * jnp.concatenate(kept, axis=1)
    upper = (iota((tokens, tokens), 0) <= iota((tokens, tokens), 1)).astype(F32)
    dlog = dot(upper, dr, 1, 0, EXACT) + at_end
    grads = (jnp.concatenate(value_dots, axis=1) - rate[...] * dlog) * jax.nn.sigmoid(pre)
    grad_dt[...] = jnp.concatenate([grads, jnp.zeros((tokens, 128 - heads), F32)], axis=1).T[:heads]

    for c in range(CHUNKS):
        z_wait(ws, e3, a3, b3, c)
        total = e3[c, 0].astype(F32)
        for k in range(1, nz):
            total = total + e3[c, k].astype(F32)
        grad_weight[:, part * c:part * c + part] = total

    for d in (1, 2, 3):
        q = (p + d) % 4
        for i in range(2):
            head_copy(ha, ga, ha_s, ha_r, i, d).wait_send()
            head_copy(hb, gb, hb_s, hb_r, i, d).wait_send()
        remote(lg.at[q], ld.at[p], lg_s.at[d - 1], lg_r.at[p], in_plane(d)).wait_send()
        for w in range(4):
            plane_copy(w, d).wait_send()
            back_copy(w, d).wait_send()
        for c in range(CHUNKS):
            y_copy(c, d).wait_send()
    pair_copy.wait_send()
    feature_copy.wait_send()

    def sent(k, _):
        peer = (z + 1 + k) % nz
        where = along_z(peer)
        remote(zl, zd.at[z], zl_s.at[peer], zl_r.at[z], where).wait_send()
        for w in range(4):
            remote(zs.at[w, peer], r2.at[w, z], s2.at[w, peer], g2.at[w, z], where).wait_send()
            remote(bk.at[w, peer], r4.at[w, z], s4.at[w, peer], g4.at[w, z], where).wait_send()
        for c in range(CHUNKS):
            remote(ws.at[c, peer], e3.at[c, z], a3.at[c, peer], b3.at[c, z], where).wait_send()
        return 0

    lax.fori_loop(0, nz - 1, sent, 0)


def deliver_kernel(*refs):
    sems = refs[8]
    copies = [pltpu.make_async_copy(refs[i], refs[4 + i], sems.at[i]) for i in range(4)]
    for copy in copies:
        copy.start()
    for copy in copies:
        copy.wait()


def deliver(outs):
    return pl.pallas_call(
        deliver_kernel,
        out_shape=tuple(jax.ShapeDtypeStruct(o.shape, o.dtype) for o in outs),
        in_specs=[VMEM] * 4,
        out_specs=(HBM,) * 4,
        scratch_shapes=[DMA((4,))],
        compiler_params=pltpu.CompilerParams(vmem_limit_bytes=8 << 20),
        name="deliver",
    )(*outs)


def per_device(values, dt_raw, dt_bias, decay_rate, features, bc_weight, out_grad):
    nz = lax.axis_size("ctx") // 4
    tokens, heads = dt_raw.shape[1:]
    feats = features.shape[2]
    two_n = bc_weight.shape[1]
    plan = scratch_plan(nz, tokens, heads, feats, two_n)
    outs = pl.pallas_call(
        make_kernel(list(plan)),
        out_shape=(
            jax.ShapeDtypeStruct(values.shape[1:], BF16),
            jax.ShapeDtypeStruct((heads, tokens), F32),
            jax.ShapeDtypeStruct((tokens, feats), BF16),
            jax.ShapeDtypeStruct((2, feats), F32),
        ),
        in_specs=[HBM] * 7,
        out_specs=(VMEM,) * 4,
        scratch_shapes=list(plan.values()),
        compiler_params=pltpu.CompilerParams(
            collective_id=0, has_side_effects=True, vmem_limit_bytes=48 << 20
        ),
        name="layer_backward",
    )(*[pltpu.with_memory_space_constraint(x, pltpu.HBM) for x in (
        values[0], dt_raw[0].T, dt_bias[None], decay_rate[None], features[0], bc_weight, out_grad[0]
    )])
    outs = deliver(outs)
    return (outs[0][None], outs[1].T[None], outs[2][None], outs[3])


def solution(mesh):
    return jax.shard_map(
        per_device,
        mesh=mesh,
        in_specs=(
            P("dp", "ctx", "head"),
            P("dp", "ctx", "head"),
            P("head"),
            P("head"),
            P("dp", "ctx", "head"),
            P("head", None),
            P("dp", "ctx", "head"),
        ),
        out_specs=(
            P("dp", "ctx", "head"),
            P("dp", "ctx", "head"),
            P("dp", "ctx", "head"),
            P(("ctx", "dp"), "head"),
        ),
        check_vma=False,
    )
```

```python
import jax
import jax.numpy as jnp
from jax import lax
from jax.experimental import pallas as pl
from jax.experimental.pallas import tpu as pltpu
from jax.sharding import PartitionSpec as P

F32 = jnp.float32
BF16 = jnp.bfloat16
EXACT = lax.Precision.HIGHEST
MESH_ID = pl.DeviceIdType.MESH
VMEM = pl.BlockSpec(memory_space=pltpu.VMEM)
HBM = pl.BlockSpec(memory_space=pltpu.HBM)
CHUNKS = 2
SIDES = 1
STREAMS = 2 * SIDES
LANES = 256 // SIDES
DMA = pltpu.SemaphoreType.DMA


def remote(src, dst, send_sem, recv_sem, where):
    return pltpu.make_async_remote_copy(
        src_ref=src, dst_ref=dst, send_sem=send_sem, recv_sem=recv_sem,
        device_id=where, device_id_type=MESH_ID,
    )


def greet(barrier, where):
    pl.semaphore_signal(barrier, inc=1, device_id=where, device_id_type=MESH_ID)


def far_first(k, nz):
    return nz // 2 + (1 - 2 * (k % 2)) * ((k + 1) // 2)


def dot(a, b, ca, cb, precision=None):
    return lax.dot_general(
        a, b, (((ca,), (cb,)), ((), ())), precision=precision, preferred_element_type=F32
    )


def iota(shape, dim):
    return lax.broadcasted_iota(jnp.int32, shape, dim)


def scratch_plan(nz, tokens, heads, feats, two_n):
    rows = 128 // nz
    part = feats // CHUNKS
    block = two_n // 8
    wide = heads * 64
    return dict(
        values=pltpu.VMEM((tokens, wide), BF16),
        raw_t=pltpu.VMEM((heads, tokens), F32),
        bias=pltpu.VMEM((1, heads), F32),
        rate=pltpu.VMEM((1, heads), F32),
        features=pltpu.VMEM((2, tokens, feats), BF16),
        weight=pltpu.VMEM((feats, two_n), BF16),
        out_grad=pltpu.VMEM((tokens, wide), BF16),
        fetched=DMA((7,)),
        relay=pltpu.SemaphoreType.REGULAR((max(nz.bit_length() - 2, 1),)),
        ha=pltpu.VMEM((2, tokens, two_n // 2), BF16),
        hb=pltpu.VMEM((2, tokens, two_n // 2), BF16),
        ga=pltpu.VMEM((2, 3, tokens, two_n // 2), BF16),
        gb=pltpu.VMEM((2, 3, tokens, two_n // 2), BF16),
        ha_s=DMA((2, 3)), ha_r=DMA((2, 3)), hb_s=DMA((2, 3)), hb_r=DMA((2, 3)),
        lg=pltpu.VMEM((4, 1, 256), F32),
        ld=pltpu.VMEM((4, 1, 256), F32),
        zl=pltpu.VMEM((1, 256), F32),
        zd=pltpu.VMEM((nz, 1, 256), F32),
        lg_s=DMA((3,)), lg_r=DMA((4,)), zl_s=DMA((nz,)), zl_r=DMA((nz,)),
        vin=pltpu.VMEM((tokens, wide), BF16),
        gin=pltpu.VMEM((tokens, wide), BF16),
        sg=pltpu.VMEM((2, 128, wide), BF16),
        r1=pltpu.VMEM((STREAMS, 4, 128, LANES), BF16),
        zs=pltpu.VMEM((STREAMS, nz, rows, LANES), BF16),
        r2=pltpu.VMEM((STREAMS, nz, rows, LANES), BF16),
        bk=pltpu.VMEM((STREAMS, nz, rows, LANES), BF16),
        r4=pltpu.VMEM((STREAMS, nz, rows, LANES), BF16),
        p5=pltpu.VMEM((STREAMS, 4, 128, LANES), BF16),
        r5=pltpu.VMEM((STREAMS, 4, 128, LANES), BF16),
        s1=DMA((STREAMS, 3)), g1=DMA((STREAMS, 4)), s2=DMA((STREAMS, nz)), g2=DMA((STREAMS, nz)),
        s4=DMA((STREAMS, nz)), g4=DMA((STREAMS, nz)), s5=DMA((STREAMS, 3)), g5=DMA((STREAMS, 4)),
        dx=pltpu.VMEM((tokens, wide), F32),
        drow=pltpu.VMEM((tokens, tokens), F32),
        pt=pltpu.VMEM((two_n, tokens), BF16),
        w1=pltpu.VMEM((CHUNKS, two_n // 2, part), F32),
        e1=pltpu.VMEM((two_n // 2, tokens), BF16),
        hs=pltpu.VMEM((CHUNKS, 3, block, part), BF16),
        e2=pltpu.VMEM((CHUNKS, 3, block, part), BF16),
        ws=pltpu.VMEM((CHUNKS, nz, 2, part), BF16),
        e3=pltpu.VMEM((CHUNKS, nz, 2, part), BF16),
        f_s=DMA((1,)), f_r=DMA((1,)), a1=DMA((1,)), b1=DMA((1,)), a2=DMA((CHUNKS, 3)), b2=DMA((CHUNKS, 3)),
        a3=DMA((CHUNKS, nz)), b3=DMA((CHUNKS, nz)),
    )


def make_kernel(names):
    def kernel(*refs):
        step(refs[:7], refs[7:11], **dict(zip(names, refs[11:])))
    return kernel


def step(held, results, *,
         values, raw_t, bias, rate, features, weight, out_grad, fetched, relay,
         ha, hb, ga, gb, ha_s, ha_r, hb_s, hb_r,
         lg, ld, zl, zd, lg_s, lg_r, zl_s, zl_r,
         vin, gin, sg, r1, zs, r2, bk, r4, p5, r5, s1, g1, s2, g2, s4, g4, s5, g5,
         dx, drow, pt, w1, e1, hs, e2, ws, e3, f_s, f_r, a1, b1, a2, b2, a3, b3):
    grad_values, grad_dt, grad_features, grad_weight = results
    here = (values, raw_t, bias, rate, features.at[0], weight, out_grad)
    fetches = [
        pltpu.make_async_copy(held[i], here[i], fetched.at[i]) for i in range(7)
    ]
    for i in (5, 4, 1, 2, 3, 0, 6):
        fetches[i].start()
    ctx, head, dp = lax.axis_index("ctx"), lax.axis_index("head"), lax.axis_index("dp")
    nz = zd.shape[0]
    z, p = ctx // 4, ctx % 4
    low, core = (ctx // 2) % 2, ctx % 2
    y = dp * 2 + low
    rows = 128 // nz
    heads, tokens = raw_t.shape
    pairs = heads // 2
    state = 128
    part = features.shape[2] // CHUNKS
    block = weight.shape[1] // 8

    def at_head(d):
        return {"head": (head + d) % 4}

    def in_plane(d):
        return {"ctx": z * 4 + (p + d) % 4}

    def along_z(peer):
        return {"ctx": peer * 4 + p}

    def along_y(d):
        to = (y + d) % 4
        return {"ctx": z * 4 + (to % 2) * 2 + core, "dp": to // 2}

    other = {"ctx": ctx + 1 - 2 * core}

    barrier = pltpu.get_barrier_semaphore()
    for d in (2, 1, 3):
        greet(barrier, at_head(d))
    for d in (1, nz - 1):
        greet(barrier, along_z((z + d) % nz))
    for d in (2, 1, 3):
        greet(barrier, along_y(d))
        greet(barrier, in_plane(d))

    fetches[5].wait()
    fetches[4].wait()
    partial = dot(features[0], weight[...], 1, 0).astype(BF16)
    ha[0] = partial[:, :state]
    ha[1] = partial[:, state:]

    pl.semaphore_wait(barrier, 11)

    reaches = [1 << i for i in range(nz.bit_length() - 2)]

    def relay_signal(i):
        for d in (reaches[i], nz - reaches[i]):
            pl.semaphore_signal(
                relay.at[i], inc=1, device_id=along_z((z + d) % nz), device_id_type=MESH_ID
            )

    def relay_wait(i):
        pl.semaphore_wait(relay.at[i], 2)

    def head_copy(src, dst, ss, rs, i, d):
        return remote(src.at[i], dst.at[i, d - 1], ss.at[i, d - 1], rs.at[i, d - 1], at_head(d))

    def head_total(src, dst, ss, rs, i):
        total = src[i].astype(F32)
        for d in (1, 3, 2):
            head_copy(src, dst, ss, rs, i, d).wait_recv()
            total = total + dst[i, d - 1].astype(F32)
        return total

    for i in range(2):
        for d in (2, 1, 3):
            head_copy(ha, ga, ha_s, ha_r, i, d).start()
    relay_signal(0)

    for i in (1, 2, 3):
        fetches[i].wait()

    def flip(few):
        return jnp.concatenate([few, jnp.zeros((128 - heads, tokens), F32)], axis=0).T[:, :heads]

    pre = flip(raw_t[...]) + bias[...]
    dt = jax.nn.softplus(pre)
    lower = (iota((tokens, tokens), 0) >= iota((tokens, tokens), 1)).astype(F32)
    run = dot(lower, -dt * rate[...], 1, 0, EXACT)
    last = run[tokens - 1:tokens, :]
    into = jnp.exp(run)
    tail = jnp.exp(last - run)
    ends = jnp.exp(last)
    run_t = jnp.concatenate([run, jnp.zeros((tokens, 128 - heads), F32)], axis=1).T
    first_half = iota((tokens, 128), 1) < 64

    def spread(cols, j):
        return jnp.where(first_half, cols[:, 2 * j:2 * j + 1], cols[:, 2 * j + 1:2 * j + 2])

    row_half = iota((1, 128), 1) < 64
    for j in range(pairs):
        lg[j // 2, :, 128 * (j % 2):128 * (j % 2) + 128] = jnp.where(
            row_half, last[:, 2 * j:2 * j + 1], last[:, 2 * j + 1:2 * j + 2]
        )
    dt_tail = dt * tail
    fetches[0].wait()
    fetches[6].wait()
    for j in range(pairs):
        lanes = slice(128 * j, 128 * j + 128)
        vin[:, lanes] = (values[:, lanes].astype(F32) * spread(dt_tail, j)).astype(BF16)
        gin[:, lanes] = (out_grad[:, lanes].astype(F32) * spread(into, j)).astype(BF16)

    for d in (2, 3, 1):
        q = (p + d) % 4
        remote(lg.at[q], ld.at[p], lg_s.at[d - 1], lg_r.at[p], in_plane(d)).start()
    for i in range(len(reaches) - 1):
        relay_wait(i)
        relay_signal(i + 1)

    def plane_copy(w, d):
        q = (p + d) % 4
        lanes = pl.ds(pl.multiple_of(q * 256 + (w % SIDES) * LANES, 128), LANES)
        return remote(sg.at[w // SIDES, :, lanes], r1.at[w, p], s1.at[w, d - 1], g1.at[w, p], in_plane(d))

    halves = []
    for i, fed in ((0, vin), (1, gin)):
        total = head_total(ha, ga, ha_s, ha_r, i)
        halves.append(total.astype(BF16))
        turned = halves[i].astype(F32).T.astype(BF16)
        sg[i] = dot(turned, fed[...], 1, 0).astype(BF16)
        for w in range(SIDES * i, SIDES * i + SIDES):
            for d in (2, 3, 1):
                plane_copy(w, d).start()
            r1[w, p] = sg[i, :, pl.ds(pl.multiple_of(p * 256 + (w % SIDES) * LANES, 128), LANES)]
    b_proj, c_proj = halves

    def plane_wait(buf, rs, ss, w):
        for d in (1, 3, 2):
            q = (p + d) % 4
            remote(buf.at[w, q], buf.at[w, q], ss.at[w, d - 1], rs.at[w, q], in_plane(d)).wait_recv()

    def lanes_of(w):
        return slice(LANES * (w % SIDES), LANES * (w % SIDES) + LANES)

    def order_of(w):
        return (0, 1, 2, 3) if w < SIDES else (3, 2, 1, 0)

    def decay_of(w, q):
        return decays[q][:, lanes_of(w)]

    def combine(w):
        order = order_of(w)
        acc = r1[w, order[0]].astype(F32)
        for q in order[1:]:
            acc = acc * decay_of(w, q) + r1[w, q].astype(F32)
        for j in range(nz):
            zs[w, j] = acc[j * rows:j * rows + rows].astype(BF16)

    def z_send(src, dst, ss, rs, w):
        def go(k, _):
            peer = (z + far_first(k, nz)) % nz
            remote(src.at[w, peer], dst.at[w, z], ss.at[w, peer], rs.at[w, z], along_z(peer)).start()
            return 0

        lax.fori_loop(0, nz - 1, go, 0)
        dst[w, z] = src[w, z]

    def z_wait(src, dst, ss, rs, w):
        def go(k, _):
            peer = (z + 1 + k) % nz
            remote(src.at[w, peer], dst.at[w, peer], ss.at[w, peer], rs.at[w, peer],
                   along_z(peer)).wait_recv()
            return 0

        lax.fori_loop(0, nz - 1, go, 0)

    ld[p] = lg[p]
    for d in (1, 2, 3):
        q = (p + d) % 4
        remote(lg.at[q], ld.at[q], lg_s.at[d - 1], lg_r.at[q], in_plane(d)).wait_recv()
    zl[...] = ld[0] + ld[1] + ld[2] + ld[3]

    relay_wait(len(reaches) - 1)

    decays = [jnp.exp(ld[q]) for q in range(4)]

    def send_decay(k, _):
        peer = (z + far_first(k, nz)) % nz
        remote(zl, zd.at[z], zl_s.at[peer], zl_r.at[z], along_z(peer)).start()
        return 0

    lax.fori_loop(0, nz - 1, send_decay, 0)
    zd[z] = zl[...]

    for w in range(STREAMS):
        plane_wait(r1, g1, s1, w)
        combine(w)
        z_send(zs, r2, s2, g2, w)

    feature_copy = remote(features.at[0], features.at[1], f_s.at[0], f_r.at[0], other)
    feature_copy.start()

    scores_t = dot(b_proj, c_proj, 1, 1)
    causal_t = iota((tokens, tokens), 0) <= iota((tokens, tokens), 1)
    strict_t = iota((tokens, tokens), 0) < iota((tokens, tokens), 1)
    strict_scores = jnp.where(strict_t, scores_t, 0.0)
    lane = iota((tokens, heads), 1)
    drow[...] = jnp.zeros_like(drow)

    def local_pairs(lo, hi, dscore, dcol):
        for j in range(lo, hi):
            lanes = slice(128 * j, 128 * j + 128)
            grads = out_grad[:, lanes]
            zero = jnp.zeros_like(grads)
            split = jnp.concatenate(
                [jnp.where(first_half, grads, zero), jnp.where(first_half, zero, grads)], axis=0
            )
            products = dot(values[:, lanes], split, 1, 1)
            mixes = []
            for i in range(2):
                h = 2 * j + i
                gap = run_t[h:h + 1, :] - run[:, h:h + 1]
                fall = jnp.exp(jnp.where(causal_t, gap, -1e30))
                mixes.append((fall * scores_t).astype(BF16))
                part = fall * (products[:, 128 * i:128 * i + 128] * dt[:, h:h + 1])
                dscore = dscore + part
                part = part * strict_scores
                drow[h:h + 1, :] = jnp.sum(part, axis=0, keepdims=True)
                dcol = jnp.where(lane == h, jnp.sum(part, axis=1, keepdims=True), dcol)
            dx[:, lanes] = dot(jnp.concatenate(mixes, axis=1), split, 1, 0)
        return dscore, dcol

    dscore = jnp.zeros((tokens, tokens), F32)
    dcol = jnp.zeros((tokens, heads), F32)
    dscore, dcol = local_pairs(0, pairs // 2, dscore, dcol)

    def owner_scan(w):
        carry = jnp.zeros((rows, LANES), F32)
        for k in range(nz):
            m = k if w < SIDES else nz - 1 - k
            bk[w, m] = carry.astype(BF16)
            carry = carry * jnp.exp(zd[m][:, lanes_of(w)]) + r2[w, m].astype(F32)

    def decay_wait(k, _):
        peer = (z + 1 + k) % nz
        remote(zl, zd.at[peer], zl_s.at[peer], zl_r.at[peer], along_z(peer)).wait_recv()
        return 0

    lax.fori_loop(0, nz - 1, decay_wait, 0)
    for w in range(STREAMS):
        z_wait(zs, r2, s2, g2, w)
        owner_scan(w)
        z_send(bk, r4, s4, g4, w)

    dscore, dcol = local_pairs(pairs // 2, pairs, dscore, dcol)
    dscore_t = dscore.astype(BF16)
    dscore_n = dscore.T.astype(BF16)
    grad_b = dot(dscore_t, c_proj, 1, 0)
    grad_c = dot(dscore_n, b_proj, 1, 0)
    dr = drow[...].T[:, :heads] - dcol

    def expand(w):
        for j in range(nz):
            span = slice(j * rows, j * rows + rows)
            carry = r4[w, j].astype(F32)
            for n, q in enumerate(order_of(w)):
                p5[w, q, span, :] = carry.astype(BF16)
                if n < 3:
                    carry = carry * decay_of(w, q) + r1[w, q, span, :].astype(F32)

    def back_copy(w, d):
        q = (p + d) % 4
        return remote(p5.at[w, q], r5.at[w, p], s5.at[w, d - 1], g5.at[w, p], in_plane(d))

    for w in range(STREAMS):
        z_wait(bk, r4, s4, g4, w)
        expand(w)
        for d in (2, 3, 1):
            back_copy(w, d).start()
        r5[w, p] = p5[w, p]

    group = (iota((256, 128), 0) // 64) == iota((256, 128), 1)
    groups = group.astype(F32)

    def head_sums(wide_rows):
        return dot(wide_rows, groups, 1, 0, EXACT)[:, :4]

    def entering(i, q):
        return jnp.concatenate([r5[SIDES * i + n, q] for n in range(SIDES)], axis=1)

    for w in range(SIDES):
        plane_wait(r5, g5, s5, w)
    for q in range(4):
        grad_c = grad_c + dot(gin[:, 256 * q:256 * q + 256], entering(0, q), 1, 1)
    hb[1] = grad_c.astype(BF16)
    for d in (2, 1, 3):
        head_copy(hb, gb, hb_s, hb_r, 1, d).start()
    for w in range(SIDES, STREAMS):
        plane_wait(r5, g5, s5, w)
    for q in range(4):
        grad_b = grad_b + dot(vin[:, 256 * q:256 * q + 256], entering(1, q), 1, 1)
    hb[0] = grad_b.astype(BF16)
    for d in (2, 1, 3):
        head_copy(hb, gb, hb_s, hb_r, 0, d).start()

    grad_cs = head_total(hb, gb, hb_s, hb_r, 1).astype(BF16)
    grad_bs = head_total(hb, gb, hb_s, hb_r, 0).astype(BF16)
    rounded = jnp.concatenate([grad_bs, grad_cs], axis=1)

    new_row = iota((2 * state, 2 * state), 0)
    inner = 2 * state // (8 * nz)
    old_row = (
        ((new_row // inner) % nz) * (8 * inner)
        + ((new_row // (inner * nz)) % 2) * (4 * inner)
        + (new_row // (4 * inner * nz)) * (2 * inner)
        + ((new_row // (2 * inner * nz)) % 2) * inner
        + new_row % inner
    )
    pick = (iota((2 * state, 2 * state), 1) == old_row).astype(BF16)
    pt[...] = dot(pick, rounded, 1, 1).astype(BF16)
    ours = pt[pl.ds(pl.multiple_of(core * state, state), state), :]
    pair_copy = remote(
        pt.at[pl.ds(pl.multiple_of((1 - core) * state, state), state)],
        e1, a1.at[0], b1.at[0], other,
    )
    pair_copy.start()

    def y_copy(c, d):
        return remote(hs.at[c, d - 1], e2.at[c, d - 1], a2.at[c, d - 1], b2.at[c, d - 1], along_y(d))

    feature_copy.wait_recv()
    pair_copy.wait_recv()
    both = jnp.concatenate([ours, e1[...]], axis=1)
    for c in range(CHUNKS):
        lanes = slice(part * c, part * c + part)
        fed = jnp.concatenate([features[0, :, lanes], features[1, :, lanes]], axis=0)
        w1[c] = dot(both, fed, 1, 0)
        for d in (2, 1, 3):
            span = pl.ds(pl.multiple_of(((y + d) % 4) * block, block), block)
            hs[c, d - 1] = w1[c, span, :].astype(BF16)
            y_copy(c, d).start()

    grad_features[...] = dot(rounded, weight[...], 1, 1).astype(BF16)

    for c in range(CHUNKS):
        span = pl.ds(pl.multiple_of(y * block, block), block)
        total = w1[c, span, :]
        for d in (1, 3, 2):
            y_copy(c, d).wait_recv()
            total = total + e2[c, d - 1].astype(F32)
        for k in range(nz):
            ws[c, k] = total[2 * k:2 * k + 2].astype(BF16)
        z_send(ws, e3, a3, b3, c)
    gains = []
    for q in range(4):
        lanes = slice(256 * q, 256 * q + 256)
        gains.append(head_sums(dot(c_proj, entering(0, q), 1, 0) * gin[:, lanes].astype(F32)))
    dr = dr + jnp.concatenate(gains, axis=1)

    falls, value_dots, kept = [], [], []
    for q in range(4):
        lanes = slice(256 * q, 256 * q + 256)
        exits = entering(1, q)
        reach = dot(b_proj, exits, 1, 0)
        falls.append(head_sums(reach * vin[:, lanes].astype(F32)))
        wide_tail = jnp.concatenate([spread(tail, 2 * q), spread(tail, 2 * q + 1)], axis=1)
        full = dx[:, lanes] + reach * wide_tail
        kept.append(head_sums(jnp.sum(
            exits.astype(F32) * entering(0, q).astype(F32), axis=0, keepdims=True
        )))
        value_dots.append(head_sums(full * values[:, lanes].astype(F32)))
        wide_dt = jnp.concatenate([spread(dt, 2 * q), spread(dt, 2 * q + 1)], axis=1)
        grad_values[:, lanes] = (full * wide_dt).astype(BF16)
    fall = jnp.concatenate(falls, axis=1)
    dr = dr - fall
    at_end = jnp.sum(fall, axis=0, keepdims=True) + ends * jnp.concatenate(kept, axis=1)
    upper = (iota((tokens, tokens), 0) <= iota((tokens, tokens), 1)).astype(F32)
    dlog = dot(upper, dr, 1, 0, EXACT) + at_end
    grads = (jnp.concatenate(value_dots, axis=1) - rate[...] * dlog) * jax.nn.sigmoid(pre)
    grad_dt[...] = jnp.concatenate([grads, jnp.zeros((tokens, 128 - heads), F32)], axis=1).T[:heads]

    for c in range(CHUNKS):
        z_wait(ws, e3, a3, b3, c)
        total = e3[c, 0].astype(F32)
        for k in range(1, nz):
            total = total + e3[c, k].astype(F32)
        grad_weight[:, part * c:part * c + part] = total

    for d in (1, 2, 3):
        q = (p + d) % 4
        for i in range(2):
            head_copy(ha, ga, ha_s, ha_r, i, d).wait_send()
            head_copy(hb, gb, hb_s, hb_r, i, d).wait_send()
        remote(lg.at[q], ld.at[p], lg_s.at[d - 1], lg_r.at[p], in_plane(d)).wait_send()
        for w in range(STREAMS):
            plane_copy(w, d).wait_send()
            back_copy(w, d).wait_send()
        for c in range(CHUNKS):
            y_copy(c, d).wait_send()
    pair_copy.wait_send()
    feature_copy.wait_send()

    def sent(k, _):
        peer = (z + 1 + k) % nz
        where = along_z(peer)
        remote(zl, zd.at[z], zl_s.at[peer], zl_r.at[z], where).wait_send()
        for w in range(STREAMS):
            remote(zs.at[w, peer], r2.at[w, z], s2.at[w, peer], g2.at[w, z], where).wait_send()
            remote(bk.at[w, peer], r4.at[w, z], s4.at[w, peer], g4.at[w, z], where).wait_send()
        for c in range(CHUNKS):
            remote(ws.at[c, peer], e3.at[c, z], a3.at[c, peer], b3.at[c, z], where).wait_send()
        return 0

    lax.fori_loop(0, nz - 1, sent, 0)


def deliver_kernel(*refs):
    sems = refs[8]
    copies = [pltpu.make_async_copy(refs[i], refs[4 + i], sems.at[i]) for i in range(4)]
    for copy in copies:
        copy.start()
    for copy in copies:
        copy.wait()


def deliver(outs):
    return pl.pallas_call(
        deliver_kernel,
        out_shape=tuple(jax.ShapeDtypeStruct(o.shape, o.dtype) for o in outs),
        in_specs=[VMEM] * 4,
        out_specs=(HBM,) * 4,
        scratch_shapes=[DMA((4,))],
        compiler_params=pltpu.CompilerParams(vmem_limit_bytes=8 << 20),
        name="deliver",
    )(*outs)


def per_device(values, dt_raw, dt_bias, decay_rate, features, bc_weight, out_grad):
    nz = lax.axis_size("ctx") // 4
    tokens, heads = dt_raw.shape[1:]
    feats = features.shape[2]
    two_n = bc_weight.shape[1]
    plan = scratch_plan(nz, tokens, heads, feats, two_n)
    outs = pl.pallas_call(
        make_kernel(list(plan)),
        out_shape=(
            jax.ShapeDtypeStruct(values.shape[1:], BF16),
            jax.ShapeDtypeStruct((heads, tokens), F32),
            jax.ShapeDtypeStruct((tokens, feats), BF16),
            jax.ShapeDtypeStruct((2, feats), F32),
        ),
        in_specs=[HBM] * 7,
        out_specs=(VMEM,) * 4,
        scratch_shapes=list(plan.values()),
        compiler_params=pltpu.CompilerParams(
            collective_id=0, has_side_effects=True, vmem_limit_bytes=48 << 20
        ),
        name="layer_backward",
    )(*[pltpu.with_memory_space_constraint(x, pltpu.HBM) for x in (
        values[0], dt_raw[0].T, dt_bias[None], decay_rate[None], features[0], bc_weight, out_grad[0]
    )])
    outs = deliver(outs)
    return (outs[0][None], outs[1].T[None], outs[2][None], outs[3])


def solution(mesh):
    return jax.shard_map(
        per_device,
        mesh=mesh,
        in_specs=(
            P("dp", "ctx", "head"),
            P("dp", "ctx", "head"),
            P("head"),
            P("head"),
            P("dp", "ctx", "head"),
            P("head", None),
            P("dp", "ctx", "head"),
        ),
        out_specs=(
            P("dp", "ctx", "head"),
            P("dp", "ctx", "head"),
            P("dp", "ctx", "head"),
            P(("ctx", "dp"), "head"),
        ),
        check_vma=False,
    )
```

```python
import jax
import jax.numpy as jnp
from jax import lax
from jax.experimental import pallas as pl
from jax.experimental.pallas import tpu as pltpu
from jax.sharding import PartitionSpec as P

F32 = jnp.float32
BF16 = jnp.bfloat16
EXACT = lax.Precision.HIGHEST
MESH_ID = pl.DeviceIdType.MESH
VMEM = pl.BlockSpec(memory_space=pltpu.VMEM)
HBM = pl.BlockSpec(memory_space=pltpu.HBM)
CHUNKS = 2
SIDES = 1
STREAMS = 2 * SIDES
LANES = 256 // SIDES
DMA = pltpu.SemaphoreType.DMA


def remote(src, dst, send_sem, recv_sem, where):
    return pltpu.make_async_remote_copy(
        src_ref=src, dst_ref=dst, send_sem=send_sem, recv_sem=recv_sem,
        device_id=where, device_id_type=MESH_ID,
    )


def greet(barrier, where):
    pl.semaphore_signal(barrier, inc=1, device_id=where, device_id_type=MESH_ID)


def far_first(k, nz):
    return nz // 2 + (1 - 2 * (k % 2)) * ((k + 1) // 2)


def dot(a, b, ca, cb, precision=None):
    return lax.dot_general(
        a, b, (((ca,), (cb,)), ((), ())), precision=precision, preferred_element_type=F32
    )


def iota(shape, dim):
    return lax.broadcasted_iota(jnp.int32, shape, dim)


def scratch_plan(nz, tokens, heads, feats, two_n):
    rows = 128 // nz
    part = feats // CHUNKS
    block = two_n // 8
    wide = heads * 64
    return dict(
        values=pltpu.VMEM((tokens, wide), BF16),
        raw_t=pltpu.VMEM((heads, tokens), F32),
        bias=pltpu.VMEM((1, heads), F32),
        rate=pltpu.VMEM((1, heads), F32),
        features=pltpu.VMEM((2, tokens, feats), BF16),
        weight=pltpu.VMEM((feats, two_n), BF16),
        out_grad=pltpu.VMEM((tokens, wide), BF16),
        fetched=DMA((9,)),
        relay=pltpu.SemaphoreType.REGULAR((max(nz.bit_length() - 2, 1),)),
        ha=pltpu.VMEM((2, tokens, two_n // 2), BF16),
        hb=pltpu.VMEM((2, tokens, two_n // 2), BF16),
        ga=pltpu.VMEM((2, 3, tokens, two_n // 2), BF16),
        gb=pltpu.VMEM((2, 3, tokens, two_n // 2), BF16),
        ha_s=DMA((2, 3)), ha_r=DMA((2, 3)), hb_s=DMA((2, 3)), hb_r=DMA((2, 3)),
        lg=pltpu.VMEM((4, 1, 256), F32),
        ld=pltpu.VMEM((4, 1, 256), F32),
        zl=pltpu.VMEM((1, 256), F32),
        zd=pltpu.VMEM((nz, 1, 256), F32),
        lg_s=DMA((3,)), lg_r=DMA((4,)), zl_s=DMA((nz,)), zl_r=DMA((nz,)),
        vin=pltpu.VMEM((tokens, wide), BF16),
        gin=pltpu.VMEM((tokens, wide), BF16),
        sg=pltpu.VMEM((2, 128, wide), BF16),
        r1=pltpu.VMEM((STREAMS, 4, 128, LANES), BF16),
        zs=pltpu.VMEM((STREAMS, nz, rows, LANES), BF16),
        r2=pltpu.VMEM((STREAMS, nz, rows, LANES), BF16),
        bk=pltpu.VMEM((STREAMS, nz, rows, LANES), BF16),
        r4=pltpu.VMEM((STREAMS, nz, rows, LANES), BF16),
        p5=pltpu.VMEM((STREAMS, 4, 128, LANES), BF16),
        r5=pltpu.VMEM((STREAMS, 4, 128, LANES), BF16),
        s1=DMA((STREAMS, 3)), g1=DMA((STREAMS, 4)), s2=DMA((STREAMS, nz)), g2=DMA((STREAMS, nz)),
        s4=DMA((STREAMS, nz)), g4=DMA((STREAMS, nz)), s5=DMA((STREAMS, 3)), g5=DMA((STREAMS, 4)),
        dx=pltpu.VMEM((tokens, wide), F32),
        drow=pltpu.VMEM((tokens, tokens), F32),
        pick=pltpu.VMEM((two_n, two_n), BF16),
        pt=pltpu.VMEM((two_n, tokens), BF16),
        w1=pltpu.VMEM((CHUNKS, two_n // 2, part), F32),
        e1=pltpu.VMEM((two_n // 2, tokens), BF16),
        hs=pltpu.VMEM((CHUNKS, 3, block, part), BF16),
        e2=pltpu.VMEM((CHUNKS, 3, block, part), BF16),
        ws=pltpu.VMEM((CHUNKS, nz, 2, part), BF16),
        e3=pltpu.VMEM((CHUNKS, nz, 2, part), BF16),
        f_s=DMA((1,)), f_r=DMA((1,)), a1=DMA((1,)), b1=DMA((1,)), a2=DMA((CHUNKS, 3)), b2=DMA((CHUNKS, 3)),
        a3=DMA((CHUNKS, nz)), b3=DMA((CHUNKS, nz)),
    )


def make_kernel(names):
    def kernel(*refs):
        step(refs[:7], refs[7:11], **dict(zip(names, refs[11:])))
    return kernel


def step(held, results, *,
         values, raw_t, bias, rate, features, weight, out_grad, fetched, relay,
         ha, hb, ga, gb, ha_s, ha_r, hb_s, hb_r,
         lg, ld, zl, zd, lg_s, lg_r, zl_s, zl_r,
         vin, gin, sg, r1, zs, r2, bk, r4, p5, r5, s1, g1, s2, g2, s4, g4, s5, g5,
         dx, drow, pick, pt, w1, e1, hs, e2, ws, e3, f_s, f_r, a1, b1, a2, b2, a3, b3):
    grad_values, grad_dt, grad_features, grad_weight = results
    here = (values, raw_t, bias, rate, features.at[0], weight, out_grad)
    fetches = {
        i: pltpu.make_async_copy(held[i], here[i], fetched.at[i]) for i in (0, 1, 2, 3, 6)
    }
    deep = weight.shape[0] // 2
    for n in range(2):
        down, across = pl.ds(deep * n, deep), pl.ds(deep * n, deep)
        fetches[4, n] = pltpu.make_async_copy(
            held[4].at[:, across], here[4].at[:, across], fetched.at[4 + 3 * n]
        )
        fetches[5, n] = pltpu.make_async_copy(
            held[5].at[down], here[5].at[down], fetched.at[5 + 3 * n]
        )
    for i in ((4, 0), (5, 0), (4, 1), (5, 1), 1, 2, 3, 0, 6):
        fetches[i].start()
    ctx, head, dp = lax.axis_index("ctx"), lax.axis_index("head"), lax.axis_index("dp")
    nz = zd.shape[0]
    z, p = ctx // 4, ctx % 4
    low, core = (ctx // 2) % 2, ctx % 2
    y = dp * 2 + low
    rows = 128 // nz
    heads, tokens = raw_t.shape
    pairs = heads // 2
    state = 128
    part = features.shape[2] // CHUNKS
    block = weight.shape[1] // 8

    def at_head(d):
        return {"head": (head + d) % 4}

    def in_plane(d):
        return {"ctx": z * 4 + (p + d) % 4}

    def along_z(peer):
        return {"ctx": peer * 4 + p}

    def along_y(d):
        to = (y + d) % 4
        return {"ctx": z * 4 + (to % 2) * 2 + core, "dp": to // 2}

    other = {"ctx": ctx + 1 - 2 * core}

    barrier = pltpu.get_barrier_semaphore()
    for d in (2, 1, 3):
        greet(barrier, at_head(d))
    for d in (1, nz - 1):
        greet(barrier, along_z((z + d) % nz))
    for d in (2, 1, 3):
        greet(barrier, along_y(d))
        greet(barrier, in_plane(d))

    sums = 0.0
    for n in range(2):
        fetches[4, n].wait()
        fetches[5, n].wait()
        span = slice(deep * n, deep * n + deep)
        sums = sums + dot(features[0, :, span], weight[span, :], 1, 0)
    partial = sums.astype(BF16)
    ha[0] = partial[:, :state]
    ha[1] = partial[:, state:]

    pl.semaphore_wait(barrier, 11)

    reaches = [1 << i for i in range(nz.bit_length() - 2)]

    def relay_signal(i):
        for d in (reaches[i], nz - reaches[i]):
            pl.semaphore_signal(
                relay.at[i], inc=1, device_id=along_z((z + d) % nz), device_id_type=MESH_ID
            )

    def relay_wait(i):
        pl.semaphore_wait(relay.at[i], 2)

    def head_copy(src, dst, ss, rs, i, d):
        return remote(src.at[i], dst.at[i, d - 1], ss.at[i, d - 1], rs.at[i, d - 1], at_head(d))

    def head_total(src, dst, ss, rs, i):
        total = src[i].astype(F32)
        for d in (1, 3, 2):
            head_copy(src, dst, ss, rs, i, d).wait_recv()
            total = total + dst[i, d - 1].astype(F32)
        return total

    for i in range(2):
        for d in (2, 1, 3):
            head_copy(ha, ga, ha_s, ha_r, i, d).start()
    relay_signal(0)

    for i in (1, 2, 3):
        fetches[i].wait()

    def flip(few):
        return jnp.concatenate([few, jnp.zeros((128 - heads, tokens), F32)], axis=0).T[:, :heads]

    pre = flip(raw_t[...]) + bias[...]
    dt = jax.nn.softplus(pre)
    lower = (iota((tokens, tokens), 0) >= iota((tokens, tokens), 1)).astype(F32)
    run = dot(lower, -dt * rate[...], 1, 0, EXACT)
    last = run[tokens - 1:tokens, :]
    into = jnp.exp(run)
    tail = jnp.exp(last - run)
    ends = jnp.exp(last)
    run_t = jnp.concatenate([run, jnp.zeros((tokens, 128 - heads), F32)], axis=1).T
    first_half = iota((tokens, 128), 1) < 64

    def spread(cols, j):
        return jnp.where(first_half, cols[:, 2 * j:2 * j + 1], cols[:, 2 * j + 1:2 * j + 2])

    row_half = iota((1, 128), 1) < 64
    for j in range(pairs):
        lg[j // 2, :, 128 * (j % 2):128 * (j % 2) + 128] = jnp.where(
            row_half, last[:, 2 * j:2 * j + 1], last[:, 2 * j + 1:2 * j + 2]
        )
    dt_tail = dt * tail
    fetches[0].wait()
    fetches[6].wait()
    for j in range(pairs):
        lanes = slice(128 * j, 128 * j + 128)
        vin[:, lanes] = (values[:, lanes].astype(F32) * spread(dt_tail, j)).astype(BF16)
        gin[:, lanes] = (out_grad[:, lanes].astype(F32) * spread(into, j)).astype(BF16)

    for d in (2, 3, 1):
        q = (p + d) % 4
        remote(lg.at[q], ld.at[p], lg_s.at[d - 1], lg_r.at[p], in_plane(d)).start()
    for i in range(len(reaches) - 1):
        relay_wait(i)
        relay_signal(i + 1)

    def plane_copy(w, d):
        q = (p + d) % 4
        lanes = pl.ds(pl.multiple_of(q * 256 + (w % SIDES) * LANES, 128), LANES)
        return remote(sg.at[w // SIDES, :, lanes], r1.at[w, p], s1.at[w, d - 1], g1.at[w, p], in_plane(d))

    halves = []
    for i, fed in ((0, vin), (1, gin)):
        total = head_total(ha, ga, ha_s, ha_r, i)
        halves.append(total.astype(BF16))
        turned = halves[i].astype(F32).T.astype(BF16)
        sg[i] = dot(turned, fed[...], 1, 0).astype(BF16)
        for w in range(SIDES * i, SIDES * i + SIDES):
            for d in (2, 3, 1):
                plane_copy(w, d).start()
            r1[w, p] = sg[i, :, pl.ds(pl.multiple_of(p * 256 + (w % SIDES) * LANES, 128), LANES)]
    b_proj, c_proj = halves

    def plane_wait(buf, rs, ss, w):
        for d in (1, 3, 2):
            q = (p + d) % 4
            remote(buf.at[w, q], buf.at[w, q], ss.at[w, d - 1], rs.at[w, q], in_plane(d)).wait_recv()

    def lanes_of(w):
        return slice(LANES * (w % SIDES), LANES * (w % SIDES) + LANES)

    def order_of(w):
        return (0, 1, 2, 3) if w < SIDES else (3, 2, 1, 0)

    def decay_of(w, q):
        return decays[q][:, lanes_of(w)]

    def combine(w):
        order = order_of(w)
        acc = r1[w, order[0]].astype(F32)
        for q in order[1:]:
            acc = acc * decay_of(w, q) + r1[w, q].astype(F32)
        for j in range(nz):
            zs[w, j] = acc[j * rows:j * rows + rows].astype(BF16)

    def z_send(src, dst, ss, rs, w):
        def go(k, _):
            peer = (z + far_first(k, nz)) % nz
            remote(src.at[w, peer], dst.at[w, z], ss.at[w, peer], rs.at[w, z], along_z(peer)).start()
            return 0

        lax.fori_loop(0, nz - 1, go, 0)
        dst[w, z] = src[w, z]

    def z_wait(src, dst, ss, rs, w):
        def go(k, _):
            peer = (z + 1 + k) % nz
            remote(src.at[w, peer], dst.at[w, peer], ss.at[w, peer], rs.at[w, peer],
                   along_z(peer)).wait_recv()
            return 0

        lax.fori_loop(0, nz - 1, go, 0)

    ld[p] = lg[p]
    for d in (1, 2, 3):
        q = (p + d) % 4
        remote(lg.at[q], ld.at[q], lg_s.at[d - 1], lg_r.at[q], in_plane(d)).wait_recv()
    zl[...] = ld[0] + ld[1] + ld[2] + ld[3]

    relay_wait(len(reaches) - 1)

    decays = [jnp.exp(ld[q]) for q in range(4)]

    def send_decay(k, _):
        peer = (z + far_first(k, nz)) % nz
        remote(zl, zd.at[z], zl_s.at[peer], zl_r.at[z], along_z(peer)).start()
        return 0

    lax.fori_loop(0, nz - 1, send_decay, 0)
    zd[z] = zl[...]

    for w in range(STREAMS):
        plane_wait(r1, g1, s1, w)
        combine(w)
        z_send(zs, r2, s2, g2, w)

    feature_copy = remote(features.at[0], features.at[1], f_s.at[0], f_r.at[0], other)
    feature_copy.start()

    scores_t = dot(b_proj, c_proj, 1, 1)
    causal_t = iota((tokens, tokens), 0) <= iota((tokens, tokens), 1)
    strict_t = iota((tokens, tokens), 0) < iota((tokens, tokens), 1)
    strict_scores = jnp.where(strict_t, scores_t, 0.0)
    lane = iota((tokens, heads), 1)
    drow[...] = jnp.zeros_like(drow)

    def local_pairs(lo, hi, dscore, dcol):
        for j in range(lo, hi):
            lanes = slice(128 * j, 128 * j + 128)
            grads = out_grad[:, lanes]
            zero = jnp.zeros_like(grads)
            split = jnp.concatenate(
                [jnp.where(first_half, grads, zero), jnp.where(first_half, zero, grads)], axis=0
            )
            products = dot(values[:, lanes], split, 1, 1)
            mixes = []
            for i in range(2):
                h = 2 * j + i
                gap = run_t[h:h + 1, :] - run[:, h:h + 1]
                fall = jnp.exp(jnp.where(causal_t, gap, -1e30))
                mixes.append((fall * scores_t).astype(BF16))
                part = fall * (products[:, 128 * i:128 * i + 128] * dt[:, h:h + 1])
                dscore = dscore + part
                part = part * strict_scores
                drow[h:h + 1, :] = jnp.sum(part, axis=0, keepdims=True)
                dcol = jnp.where(lane == h, jnp.sum(part, axis=1, keepdims=True), dcol)
            dx[:, lanes] = dot(jnp.concatenate(mixes, axis=1), split, 1, 0)
        return dscore, dcol

    dscore = jnp.zeros((tokens, tokens), F32)
    dcol = jnp.zeros((tokens, heads), F32)
    dscore, dcol = local_pairs(0, pairs // 2, dscore, dcol)

    def owner_scan(w):
        carry = jnp.zeros((rows, LANES), F32)
        for k in range(nz):
            m = k if w < SIDES else nz - 1 - k
            bk[w, m] = carry.astype(BF16)
            carry = carry * jnp.exp(zd[m][:, lanes_of(w)]) + r2[w, m].astype(F32)

    def decay_wait(k, _):
        peer = (z + 1 + k) % nz
        remote(zl, zd.at[peer], zl_s.at[peer], zl_r.at[peer], along_z(peer)).wait_recv()
        return 0

    lax.fori_loop(0, nz - 1, decay_wait, 0)
    for w in range(STREAMS):
        z_wait(zs, r2, s2, g2, w)
        owner_scan(w)
        z_send(bk, r4, s4, g4, w)

    dscore, dcol = local_pairs(pairs // 2, pairs, dscore, dcol)
    dscore_t = dscore.astype(BF16)
    dscore_n = dscore.T.astype(BF16)
    grad_b = dot(dscore_t, c_proj, 1, 0)
    grad_c = dot(dscore_n, b_proj, 1, 0)
    dr = drow[...].T[:, :heads] - dcol

    new_row = iota((2 * state, 2 * state), 0)
    inner = 2 * state // (8 * nz)
    old_row = (
        ((new_row // inner) % nz) * (8 * inner)
        + ((new_row // (inner * nz)) % 2) * (4 * inner)
        + (new_row // (4 * inner * nz)) * (2 * inner)
        + ((new_row // (2 * inner * nz)) % 2) * inner
        + new_row % inner
    )
    pick[...] = (iota((2 * state, 2 * state), 1) == old_row).astype(BF16)

    def expand(w):
        for j in range(nz):
            span = slice(j * rows, j * rows + rows)
            carry = r4[w, j].astype(F32)
            for n, q in enumerate(order_of(w)):
                p5[w, q, span, :] = carry.astype(BF16)
                if n < 3:
                    carry = carry * decay_of(w, q) + r1[w, q, span, :].astype(F32)

    def back_copy(w, d):
        q = (p + d) % 4
        return remote(p5.at[w, q], r5.at[w, p], s5.at[w, d - 1], g5.at[w, p], in_plane(d))

    for w in range(STREAMS):
        z_wait(bk, r4, s4, g4, w)
        expand(w)
        for d in (2, 3, 1):
            back_copy(w, d).start()
        r5[w, p] = p5[w, p]

    group = (iota((256, 128), 0) // 64) == iota((256, 128), 1)
    groups = group.astype(F32)

    def head_sums(wide_rows):
        return dot(wide_rows, groups, 1, 0, EXACT)[:, :4]

    def entering(i, q):
        return jnp.concatenate([r5[SIDES * i + n, q] for n in range(SIDES)], axis=1)

    for w in range(SIDES):
        plane_wait(r5, g5, s5, w)
    for q in range(4):
        grad_c = grad_c + dot(gin[:, 256 * q:256 * q + 256], entering(0, q), 1, 1)
    hb[1] = grad_c.astype(BF16)
    for d in (2, 1, 3):
        head_copy(hb, gb, hb_s, hb_r, 1, d).start()
    for w in range(SIDES, STREAMS):
        plane_wait(r5, g5, s5, w)
    for q in range(4):
        grad_b = grad_b + dot(vin[:, 256 * q:256 * q + 256], entering(1, q), 1, 1)
    hb[0] = grad_b.astype(BF16)
    for d in (2, 1, 3):
        head_copy(hb, gb, hb_s, hb_r, 0, d).start()

    grad_cs = head_total(hb, gb, hb_s, hb_r, 1).astype(BF16)
    picked = dot(pick[:, state:], grad_cs, 1, 1)
    grad_bs = head_total(hb, gb, hb_s, hb_r, 0).astype(BF16)
    rounded = jnp.concatenate([grad_bs, grad_cs], axis=1)

    pt[...] = (picked + dot(pick[:, :state], grad_bs, 1, 1)).astype(BF16)
    ours = pt[pl.ds(pl.multiple_of(core * state, state), state), :]
    pair_copy = remote(
        pt.at[pl.ds(pl.multiple_of((1 - core) * state, state), state)],
        e1, a1.at[0], b1.at[0], other,
    )
    pair_copy.start()

    def y_copy(c, d):
        return remote(hs.at[c, d - 1], e2.at[c, d - 1], a2.at[c, d - 1], b2.at[c, d - 1], along_y(d))

    feature_copy.wait_recv()
    pair_copy.wait_recv()
    both = jnp.concatenate([ours, e1[...]], axis=1)
    for c in range(CHUNKS):
        lanes = slice(part * c, part * c + part)
        fed = jnp.concatenate([features[0, :, lanes], features[1, :, lanes]], axis=0)
        w1[c] = dot(both, fed, 1, 0)
        for d in (2, 1, 3):
            span = pl.ds(pl.multiple_of(((y + d) % 4) * block, block), block)
            hs[c, d - 1] = w1[c, span, :].astype(BF16)
            y_copy(c, d).start()

    grad_features[...] = dot(rounded, weight[...], 1, 1).astype(BF16)

    for c in range(CHUNKS):
        span = pl.ds(pl.multiple_of(y * block, block), block)
        total = w1[c, span, :]
        for d in (1, 3, 2):
            y_copy(c, d).wait_recv()
            total = total + e2[c, d - 1].astype(F32)
        for k in range(nz):
            ws[c, k] = total[2 * k:2 * k + 2].astype(BF16)
        z_send(ws, e3, a3, b3, c)
    gains = []
    for q in range(4):
        lanes = slice(256 * q, 256 * q + 256)
        gains.append(head_sums(dot(c_proj, entering(0, q), 1, 0) * gin[:, lanes].astype(F32)))
    dr = dr + jnp.concatenate(gains, axis=1)

    falls, value_dots, kept = [], [], []
    for q in range(4):
        lanes = slice(256 * q, 256 * q + 256)
        exits = entering(1, q)
        reach = dot(b_proj, exits, 1, 0)
        falls.append(head_sums(reach * vin[:, lanes].astype(F32)))
        wide_tail = jnp.concatenate([spread(tail, 2 * q), spread(tail, 2 * q + 1)], axis=1)
        full = dx[:, lanes] + reach * wide_tail
        kept.append(head_sums(jnp.sum(
            exits.astype(F32) * entering(0, q).astype(F32), axis=0, keepdims=True
        )))
        value_dots.append(head_sums(full * values[:, lanes].astype(F32)))
        wide_dt = jnp.concatenate([spread(dt, 2 * q), spread(dt, 2 * q + 1)], axis=1)
        grad_values[:, lanes] = (full * wide_dt).astype(BF16)
    fall = jnp.concatenate(falls, axis=1)
    dr = dr - fall
    at_end = jnp.sum(fall, axis=0, keepdims=True) + ends * jnp.concatenate(kept, axis=1)
    upper = (iota((tokens, tokens), 0) <= iota((tokens, tokens), 1)).astype(F32)
    dlog = dot(upper, dr, 1, 0, EXACT) + at_end
    grads = (jnp.concatenate(value_dots, axis=1) - rate[...] * dlog) * jax.nn.sigmoid(pre)
    grad_dt[...] = jnp.concatenate([grads, jnp.zeros((tokens, 128 - heads), F32)], axis=1).T[:heads]

    for c in range(CHUNKS):
        z_wait(ws, e3, a3, b3, c)
        total = e3[c, 0].astype(F32)
        for k in range(1, nz):
            total = total + e3[c, k].astype(F32)
        grad_weight[:, part * c:part * c + part] = total

    for d in (1, 2, 3):
        q = (p + d) % 4
        for i in range(2):
            head_copy(ha, ga, ha_s, ha_r, i, d).wait_send()
            head_copy(hb, gb, hb_s, hb_r, i, d).wait_send()
        remote(lg.at[q], ld.at[p], lg_s.at[d - 1], lg_r.at[p], in_plane(d)).wait_send()
        for w in range(STREAMS):
            plane_copy(w, d).wait_send()
            back_copy(w, d).wait_send()
        for c in range(CHUNKS):
            y_copy(c, d).wait_send()
    pair_copy.wait_send()
    feature_copy.wait_send()

    def sent(k, _):
        peer = (z + 1 + k) % nz
        where = along_z(peer)
        remote(zl, zd.at[z], zl_s.at[peer], zl_r.at[z], where).wait_send()
        for w in range(STREAMS):
            remote(zs.at[w, peer], r2.at[w, z], s2.at[w, peer], g2.at[w, z], where).wait_send()
            remote(bk.at[w, peer], r4.at[w, z], s4.at[w, peer], g4.at[w, z], where).wait_send()
        for c in range(CHUNKS):
            remote(ws.at[c, peer], e3.at[c, z], a3.at[c, peer], b3.at[c, z], where).wait_send()
        return 0

    lax.fori_loop(0, nz - 1, sent, 0)


def deliver_kernel(*refs):
    sems = refs[8]
    copies = [pltpu.make_async_copy(refs[i], refs[4 + i], sems.at[i]) for i in range(4)]
    for copy in copies:
        copy.start()
    for copy in copies:
        copy.wait()


def deliver(outs):
    return pl.pallas_call(
        deliver_kernel,
        out_shape=tuple(jax.ShapeDtypeStruct(o.shape, o.dtype) for o in outs),
        in_specs=[VMEM] * 4,
        out_specs=(HBM,) * 4,
        scratch_shapes=[DMA((4,))],
        compiler_params=pltpu.CompilerParams(vmem_limit_bytes=8 << 20),
        name="deliver",
    )(*outs)


def per_device(values, dt_raw, dt_bias, decay_rate, features, bc_weight, out_grad):
    nz = lax.axis_size("ctx") // 4
    tokens, heads = dt_raw.shape[1:]
    feats = features.shape[2]
    two_n = bc_weight.shape[1]
    plan = scratch_plan(nz, tokens, heads, feats, two_n)
    outs = pl.pallas_call(
        make_kernel(list(plan)),
        out_shape=(
            jax.ShapeDtypeStruct(values.shape[1:], BF16),
            jax.ShapeDtypeStruct((heads, tokens), F32),
            jax.ShapeDtypeStruct((tokens, feats), BF16),
            jax.ShapeDtypeStruct((2, feats), F32),
        ),
        in_specs=[HBM] * 7,
        out_specs=(VMEM,) * 4,
        scratch_shapes=list(plan.values()),
        compiler_params=pltpu.CompilerParams(
            collective_id=0, has_side_effects=True, vmem_limit_bytes=48 << 20
        ),
        name="layer_backward",
    )(*[pltpu.with_memory_space_constraint(x, pltpu.HBM) for x in (
        values[0], dt_raw[0].T, dt_bias[None], decay_rate[None], features[0], bc_weight, out_grad[0]
    )])
    outs = deliver(outs)
    return (outs[0][None], outs[1].T[None], outs[2][None], outs[3])


def solution(mesh):
    return jax.shard_map(
        per_device,
        mesh=mesh,
        in_specs=(
            P("dp", "ctx", "head"),
            P("dp", "ctx", "head"),
            P("head"),
            P("head"),
            P("dp", "ctx", "head"),
            P("head", None),
            P("dp", "ctx", "head"),
        ),
        out_specs=(
            P("dp", "ctx", "head"),
            P("dp", "ctx", "head"),
            P("dp", "ctx", "head"),
            P(("ctx", "dp"), "head"),
        ),
        check_vma=False,
    )
```
